128 devices in a mesh: seq: 32 (over z, x, core), dp: 4 (over y).
Axes of the slice: x: 4, y: 4, z: 4, core: 2. Of those that a mesh axis runs over, the one named last changes fastest.
Arguments:
- features: bfloat16 [131072, 768], P(('dp', 'seq')), parts along dimension 0, may hold values from -6 to 6
- conv_one: bfloat16 [5, 768, 896], replicated, may hold values from -0.09375 to 0.09375
- conv_two: bfloat16 [5, 896, 1024], replicated, may hold values from -0.09375 to 0.09375
- head_vector: float32 [1024], replicated, may hold values from -5 to 5
- owner_of: int32 [32768, 1], P(('dp', 'seq')), parts along dimension 0, may hold values from 0 to 31; in each aligned block of 256 rows (0 to 255, 256 to 511, ...) at most 16 rows name the same one
- donor_row: int32 [32768], P(('dp', 'seq')), parts along dimension 0, may hold values from 0 to 255
- accept_row: int32 [32768], P(('dp', 'seq')), parts along dimension 0, may hold values from 0 to 255
- score_grad: bfloat16 [32768], P(('dp', 'seq')), parts along dimension 0, may hold values from -6 to 6
Outputs:
- grad_one: float32 [3584, 5, 768], P(('dp', 'seq')), parts along dimension 0
- grad_two: float32 [4096, 5, 896], P(('dp', 'seq')), parts along dimension 0
The draws below stay inside these ranges and needn't reach their ends.
There are 4 independent parts, one for each index of `dp`. The reference program is written for one: setup_inputs(seed, part) draws one part's arguments, and reference() takes and returns one part's arrays. A program takes and returns all parts, laid end to end along the dimension named above; an argument that names none is the same for every part. Nothing has to cross between parts.
Inputs may be any that keep to these rules, and one draw needn't show every extreme that they name: `owner_of`: among the 256 junction records of one device no owner is named more than 16 times, and in some device's records one owner exactly 16 times.
All inputs are finite; a program needn't handle non-finite values.
Results may differ from the reference program's by a relative error of at most 0.0056.
Values may be sent and summed in bfloat16 or wider, within the bound.
No kernel may reach another device: no remote copies, remote signals or barrier semaphores. Data moves between devices by JAX's collectives and lax.ppermute only.
A program may use at most 192 MiB of HBM per device.

```python
import math
import jax
import jax.numpy as jnp
import numpy as np
from jax import lax

C0 = 768
C1 = 896
C2 = 1024
KW = 5
J_DEV = 256
ROWS_C = 256
LENGTH = 32768
JUNCS = 8192
CAP = 16
N_SEQ = 32


def plant(drawn, own_key, low, top_value):
    place = [jax.random.randint(jax.random.fold_in(own_key, axis), (), 0, length) for axis, length in enumerate(drawn.shape)]
    main_axis = drawn.shape.index(max(drawn.shape))
    neighbour = place[:main_axis] + [(place[main_axis] + 1) % drawn.shape[main_axis]] + place[main_axis + 1:]
    return drawn.at[tuple(place)].set(low).at[tuple(neighbour)].set(top_value)


def levels(rng, dims, shards, smallest, largest):
    gain, own = 1.0, jax.random.fold_in(rng, 6)
    for dim, blocks in shards:
        heights = jnp.exp(jax.random.uniform(jax.random.fold_in(own, dim), (blocks,), jnp.float32, smallest / len(shards), largest / len(shards)))
        gain = gain * jnp.repeat(heights, dims[dim] // blocks).reshape([-1 if axis == dim else 1 for axis in range(len(dims))])
    return gain


def deal_out(rng, own, number, rows, number_of, top, bound, slope):
    sequence = jax.random.permutation(rng, number_of)
    heavy_load, common = load_shares(number_of, rows * top, bound, slope, True), load_shares(number_of, rows * top, bound, slope, False)
    places = jnp.arange(number_of)

    def named(lengths, offset_by):
        used = int((lengths > 0).sum())
        fixed = max(1, used // 4)
        moved = fixed + (places - fixed + offset_by * (used - fixed)) % max(1, number_of - fixed)
        return jnp.zeros((number_of,), jnp.int32).at[sequence[jnp.where(places < fixed, places, moved)]].set(jnp.asarray(lengths, jnp.int32))

    lengths = jnp.where(number % 4 == 0, named(heavy_load, number // 4), named(common, number - number // 4 - 1))
    mixed = jax.random.permutation(jax.random.fold_in(own, 3), number_of)
    giver, sink = mixed[0:number_of // 2 * 2:2], mixed[1:number_of // 2 * 2:2]
    room = jnp.minimum(lengths[giver] - 1, bound - lengths[sink]) // 2
    room = jnp.where((giver == sequence[0]) | (sink == sequence[0]) | (lengths[sink] == 0), 0, jnp.maximum(room, 0))
    moved = jax.random.randint(jax.random.fold_in(own, 4), (number_of // 2,), 0, 1 << 20) % (room + 1)
    lengths = lengths.at[giver].add(-moved).at[sink].add(moved)
    members = jnp.searchsorted(jnp.cumsum(lengths), jnp.arange(rows * top), side="right").astype(jnp.int32)
    listing = members.reshape(top, rows).T
    listing = listing[jax.random.permutation(jax.random.fold_in(own, 1), rows)]
    offset_by = jax.random.randint(jax.random.fold_in(own, 2), (rows, 1), 0, top)
    return jnp.take_along_axis(listing, (jnp.arange(top)[None, :] + offset_by) % top, axis=1)


def load_shares(count, total, reach, lean, full):
    weights = [(1 << 20) // math.isqrt(standing ** lean) + 1 for standing in range(1, count + 1)]
    largest = reach if full else min(reach, max(-(-total // count), total * weights[0] // sum(weights)))
    least = 1 if total - largest >= count - 1 else 0
    given, spare = [largest] + [least] * (count - 1), total - largest - least * (count - 1)
    while spare > 0:
        free = [i for i in range(1, count) if given[i] < largest] or [i for i in range(1, count) if given[i] < reach]
        pool, budget = sum([weights[i] for i in free]), spare
        for i in free:
            more = min(reach - given[i], max(1, budget * weights[i] // pool), spare)
            given[i] = given[i] + more
            spare = spare - more
    return np.array(given)


def scatter_about(rng, extent, width, reach, split=(), kind=jnp.bfloat16):
    entries = width * jax.random.normal(rng, extent, jnp.float32)
    if split:
        entries = entries * levels(rng, extent, split, -0.22, 0.18)
    return jnp.clip(entries, -reach, reach).astype(kind)


def setup_inputs(seed: int = 0, part: int = 0) -> dict:
    key_list = jax.random.split(jax.random.key(seed), 9)
    part_splits = jax.random.split(jax.random.fold_in(key_list[8], part), 9)
    features = scatter_about(part_splits[0], (LENGTH, C0), 1.0, 6.0, ((0, 32),))
    conv_one = scatter_about(key_list[1], (KW, C0, C1), (KW * C0) ** -0.5, 0.09375)
    conv_two = scatter_about(key_list[2], (KW, C1, C2), (KW * C1) ** -0.5, 0.09375)
    head_vector = scatter_about(key_list[3], (C2,), 1.0, 5.0, (), jnp.float32)
    owner_of_keys = jax.random.split(jax.random.fold_in(part_splits[4], 1), JUNCS // J_DEV)
    owner_of_turns = jax.random.permutation(jax.random.fold_in(part_splits[4], 3), JUNCS // J_DEV)
    owner_of = jax.vmap(lambda own, number: deal_out(jax.random.fold_in(part_splits[4], 2), own, number, J_DEV, N_SEQ, 1, CAP, 2))(owner_of_keys, owner_of_turns).reshape((JUNCS, 1))
    donor_row = plant(jax.random.randint(part_splits[5], (JUNCS,), 0, ROWS_C), jax.random.fold_in(part_splits[5], 1), 0, ROWS_C - 1).astype(jnp.int32)
    accept_row = plant(jax.random.randint(part_splits[6], (JUNCS,), 0, ROWS_C), jax.random.fold_in(part_splits[6], 1), 0, ROWS_C - 1).astype(jnp.int32)
    score_grad = scatter_about(part_splits[7], (JUNCS,), 1.0, 6.0, ((0, 32),))
    return {"features": features, "conv_one": conv_one, "conv_two": conv_two, "head_vector": head_vector, "owner_of": owner_of, "donor_row": donor_row, "accept_row": accept_row, "score_grad": score_grad}


def gelu_fn(value):
    return jax.nn.gelu(value, approximate=True)

def gelu_back(value, upstream):
    return jax.vjp(gelu_fn, value)[1](upstream)[0]

def convolve(inputs, weight):
    half = weight.shape[0] // 2
    count = inputs.shape[0]
    padded = jnp.pad(inputs, ((half, half), (0, 0)))
    total = jnp.zeros((count, weight.shape[2]), jnp.float32)
    for tap_index in range(weight.shape[0]):
        total = total + jnp.dot(padded[tap_index:tap_index + count], weight[tap_index], preferred_element_type=jnp.float32)
    return total

def transpose_conv(grads, weight):
    half = weight.shape[0] // 2
    count = grads.shape[0]
    padded = jnp.pad(grads, ((half, half), (0, 0)))
    total = jnp.zeros((count, weight.shape[1]), jnp.float32)
    for tap_index in range(weight.shape[0]):
        window = padded[2 * half - tap_index:2 * half - tap_index + count]
        total = total + lax.dot_general(window, weight[tap_index], (((1,), (1,)), ((), ())), preferred_element_type=jnp.float32)
    return total

def weight_terms(inputs, grads, taps):
    half = taps // 2
    count = inputs.shape[0]
    padded = jnp.pad(inputs, ((half, half), (0, 0)))
    parts = [lax.dot_general(grads, padded[tap_index:tap_index + count], (((0,), (0,)), ((), ())), preferred_element_type=jnp.float32) for tap_index in range(taps)]
    return jnp.stack(parts, 1)

def pool_pairs(hidden):
    return hidden.reshape(hidden.shape[0] // 2, 2, hidden.shape[1]).mean(axis=1).astype(jnp.bfloat16)

def spread_pairs(grads):
    return jnp.repeat(grads, 2, axis=0) * 0.5

def reference(features, conv_one, conv_two, head_vector, owner_of, donor_row, accept_row, score_grad):
    pre_one = convolve(features, conv_one)
    pooled_one = pool_pairs(gelu_fn(pre_one))
    pre_two = convolve(pooled_one, conv_two)
    embed = pool_pairs(gelu_fn(pre_two))
    holder = (jnp.arange(JUNCS, dtype=jnp.int32) // J_DEV).astype(jnp.int32)
    donors = owner_of[:, 0] * ROWS_C + donor_row
    acceptors = holder * ROWS_C + accept_row
    donor_vals = embed[donors].astype(jnp.float32)
    accept_vals = embed[acceptors].astype(jnp.float32)
    coef = score_grad.astype(jnp.float32)[:, None] * head_vector[None, :]
    embed_grad = jnp.zeros(embed.shape, jnp.float32)
    embed_grad = embed_grad.at[donors].add(coef * accept_vals)
    embed_grad = embed_grad.at[acceptors].add(coef * donor_vals)
    grad_pre_two = gelu_back(pre_two, spread_pairs(embed_grad)).astype(jnp.bfloat16)
    grad_two = weight_terms(pooled_one, grad_pre_two, KW)
    grad_pool = transpose_conv(grad_pre_two, conv_two)
    grad_pre_one = gelu_back(pre_one, spread_pairs(grad_pool)).astype(jnp.bfloat16)
    grad_one = weight_terms(features, grad_pre_one, KW)
    return (grad_one, grad_two)
```

```python
import functools

import jax
import jax.numpy as jnp
from jax import lax
from jax.experimental import pallas as pl
from jax.experimental.pallas import tpu as pltpu
from jax.sharding import PartitionSpec as P

NZ, NX = 4, 4
BF = jnp.bfloat16
F32 = jnp.float32


def index_of(z, x, c):
    return ((z % NZ) * NX + (x % NX)) * 2 + c


def pairs_of(move):
    return [
        (index_of(z, x, c), index_of(*move(z, x, c)))
        for z in range(NZ)
        for x in range(NX)
        for c in range(2)
    ]


SIBLING = pairs_of(lambda z, x, c: (z, x, 1 - c))
RINGS = (
    (
        pairs_of(lambda z, x, c: (z, x + 1, c) if c == 0 else (z + 1, x, c)),
        pairs_of(lambda z, x, c: (z, x - 1, c) if c == 0 else (z - 1, x, c)),
    ),
    (
        pairs_of(lambda z, x, c: (z + 1, x, c) if c == 0 else (z, x + 1, c)),
        pairs_of(lambda z, x, c: (z - 1, x, c) if c == 0 else (z, x - 1, c)),
    ),
)
N_SEQ = NZ * NX * 2
OUTWARD = [(s, s - 1) for s in range(2, N_SEQ, 2)] + [(s, s + 1) for s in range(1, N_SEQ - 1, 2)]


def move(value, pairs):
    return lax.ppermute(value, "seq", pairs)


VM = pltpu.VMEM
IN_VMEM = pl.BlockSpec(memory_space=pltpu.VMEM)
IN_PLACE = pl.BlockSpec(memory_space=pl.ANY)
LANES = 128
PIECE = 128
TILE = 256
RIM = 16


def params(mib=44):
    return pltpu.CompilerParams(vmem_limit_bytes=mib << 20)


def cost(flops, bytes_accessed, transcendentals=0):
    return pl.CostEstimate(
        flops=flops, bytes_accessed=bytes_accessed, transcendentals=transcendentals
    )


def gelu_both(v):
    c, a = 0.7978845608028654, 0.044715
    sq = v * v
    t = jnp.tanh(c * v * (1.0 + a * sq))
    up = 0.5 * (1.0 + t)
    return v * up, up + 0.5 * v * (1.0 - t * t) * (c * (1.0 + 3.0 * a * sq))


def fill_rims(rimmed, block_ref, rim_ref):
    n = block_ref.shape[0]
    rimmed[0:RIM] = rim_ref[0:RIM]
    rimmed[RIM : RIM + n] = block_ref[...]
    rimmed[RIM + n : 2 * RIM + n] = rim_ref[RIM : 2 * RIM]


def conv_kernel(
    taps, x_ref, rim_ref, w_hbm, pooled_ref, even_ref, odd_ref, w_ref, rimmed, piece, wide, acc, sem
):
    n, f = x_ref.shape
    copies = [
        pltpu.make_async_copy(w_hbm.at[k], w_ref.at[pl.ds(k * f, f)], sem.at[k])
        for k in range(taps)
    ]
    for copy in copies:
        copy.start()
    fill_rims(rimmed, x_ref, rim_ref)

    @pl.loop(0, n // PIECE)
    def _(m):
        r = pl.multiple_of(m * PIECE, PIECE)
        piece[...] = rimmed[pl.ds(r, PIECE + 2 * RIM), :].astype(F32)
        for k in range(taps):
            low = RIM - taps // 2 + k
            wide[pl.ds(r, PIECE), k * f : (k + 1) * f] = piece[low : low + PIECE, :].astype(BF)

    for copy in copies:
        copy.wait()

    @pl.loop(0, n // TILE)
    def _(m):
        r = pl.multiple_of(m * TILE, TILE)
        q = pl.ds(pl.multiple_of(m * (TILE // 2), TILE // 2), TILE // 2)
        total = jnp.dot(wide[pl.ds(r, TILE), :], w_ref[...], preferred_element_type=F32)
        for j in range(acc.shape[0]):
            cols = slice(j * LANES, (j + 1) * LANES)
            acc[j] = total[:, cols]
            even, even_slope = gelu_both(acc[j, pl.ds(0, TILE // 2, stride=2), :])
            odd, odd_slope = gelu_both(acc[j, pl.ds(1, TILE // 2, stride=2), :])
            pooled_ref[q, cols] = ((even + odd) * 0.5).astype(BF)
            even_ref[q, cols] = even_slope * 0.5
            odd_ref[q, cols] = odd_slope * 0.5


def conv_pool(x, rim, w):
    taps, f, c = w.shape
    n = x.shape[0]
    return pl.pallas_call(
        functools.partial(conv_kernel, taps),
        out_shape=[jax.ShapeDtypeStruct((n // 2, c), BF)]
        + [jax.ShapeDtypeStruct((n // 2, c), F32)] * 2,
        in_specs=[IN_VMEM, IN_VMEM, IN_PLACE],
        out_specs=[IN_VMEM] * 3,
        scratch_shapes=[
            VM((taps * f, c), BF),
            VM((n + 2 * RIM, f), BF),
            VM((PIECE + 2 * RIM, f), F32),
            VM((n, taps * f), BF),
            VM((c // LANES, TILE, LANES), F32),
            pltpu.SemaphoreType.DMA((taps,)),
        ],
        compiler_params=params(),
        cost_estimate=cost(2 * n * f * c * taps, 2 * (n * f + taps * f * c) + 5 * n * c, n * c),
        name="conv_pool",
    )(x, rim, w)


def back_kernel(
    taps, g_ref, rim_ref, w_hbm, even_ref, odd_ref, order_ref, out_ref, w_ref, rimmed, piece, wide, pairs, flat, sem
):
    n = g_ref.shape[0]
    copies = [pltpu.make_async_copy(w_hbm.at[k], w_ref.at[k], sem.at[k]) for k in range(taps)]
    for copy in copies:
        copy.start()
    fill_rims(rimmed, g_ref, rim_ref)

    @pl.loop(0, n // PIECE)
    def _(m):
        r = pl.multiple_of(m * PIECE, PIECE)
        piece[...] = rimmed[pl.ds(r, PIECE + 2 * RIM), :].astype(F32)
        for k in range(taps):
            low = RIM + taps // 2 - k
            wide[k, pl.ds(r, PIECE), :] = piece[low : low + PIECE, :].astype(BF)

    for copy in copies:
        copy.wait()

    @pl.loop(0, n // TILE)
    def _(m):
        r = pl.multiple_of(m * TILE, TILE)
        rows = pl.ds(r, TILE)
        total = sum(
            lax.dot_general(
                wide[k, rows, :], w_ref[k], (((1,), (1,)), ((), ())), preferred_element_type=F32
            )
            for k in range(taps)
        )
        for j in range(pairs.shape[0]):
            cols = slice(j * LANES, (j + 1) * LANES)
            pairs[j, pl.ds(0, TILE, stride=2), :] = total[:, cols] * even_ref[rows, cols]
            pairs[j, pl.ds(1, TILE, stride=2), :] = total[:, cols] * odd_ref[rows, cols]
            flat[:, cols] = pairs[j].astype(BF)
        turned = lax.dot_general(
            order_ref[...], flat[...], (((1,), (1,)), ((), ())), preferred_element_type=F32
        )
        out_ref[:, pl.ds(pl.multiple_of(2 * r, 2 * TILE), 2 * TILE)] = turned.astype(BF)


def conv_back(g, rim, w, even, odd, order):
    taps, f, c = w.shape
    n = g.shape[0]
    return pl.pallas_call(
        functools.partial(back_kernel, taps),
        out_shape=jax.ShapeDtypeStruct((f, 2 * n), BF),
        in_specs=[IN_VMEM, IN_VMEM, IN_PLACE, IN_VMEM, IN_VMEM, IN_VMEM],
        out_specs=IN_VMEM,
        scratch_shapes=[
            VM((taps, f, c), BF),
            VM((n + 2 * RIM, c), BF),
            VM((PIECE + 2 * RIM, c), F32),
            VM((taps, n, c), BF),
            VM((f // LANES, 2 * TILE, LANES), F32),
            VM((2 * TILE, f), BF),
            pltpu.SemaphoreType.DMA((taps,)),
        ],
        compiler_params=params(),
        cost_estimate=cost(
            2 * n * f * c * taps + 4 * n * f * f, 2 * (n * c + taps * f * c + f * f) + 12 * n * f
        ),
        name="conv_back",
    )(g, rim, w, even, odd, order)


def head_kernel(add_ref, come_ref, head_ref, even_ref, odd_ref, order_ref, g_ref, turned_ref, pairs):
    n = add_ref.shape[0]
    total = jnp.dot(add_ref[...], come_ref[...], preferred_element_type=F32) * head_ref[...]
    for j in range(pairs.shape[0]):
        cols = slice(j * LANES, (j + 1) * LANES)
        pairs[j, pl.ds(0, n, stride=2), :] = total[:, cols] * even_ref[:, cols]
        pairs[j, pl.ds(1, n, stride=2), :] = total[:, cols] * odd_ref[:, cols]
        g_ref[:, cols] = pairs[j].astype(BF)
    turned_ref[...] = lax.dot_general(
        order_ref[...], g_ref[...], (((1,), (1,)), ((), ())), preferred_element_type=F32
    ).astype(BF)


def head_back(add, come, head, even, odd, order):
    n, c = even.shape
    return pl.pallas_call(
        head_kernel,
        out_shape=[jax.ShapeDtypeStruct((2 * n, c), BF), jax.ShapeDtypeStruct((c, 2 * n), BF)],
        in_specs=[IN_VMEM] * 6,
        out_specs=[IN_VMEM] * 2,
        scratch_shapes=[VM((c // LANES, 2 * n, LANES), F32)],
        compiler_params=params(),
        cost_estimate=cost(
            2 * n * c * come.shape[0] + 4 * n * c * c, 2 * (come.size + add.size + c * c) + 16 * n * c
        ),
        name="head_back",
    )(add, come, head, even, odd, order)


def window_kernel(taps, own_ref, own_rim, other_ref, other_rim, out_ref, rimmed, piece):
    n = own_ref.shape[0]
    step = pl.program_id(0)

    @pl.when(step == 0)
    def _():
        fill_rims(rimmed.at[0], own_ref, own_rim)
        fill_rims(rimmed.at[1], other_ref, other_rim)

    per = n // PIECE
    side, m = step // per, step % per
    r = pl.multiple_of(m * PIECE, PIECE)
    piece[...] = rimmed[side, pl.ds(r, PIECE + 2 * RIM), :].astype(F32)
    for k in range(taps):
        low = RIM - taps // 2 + k
        out_ref[k] = piece[low : low + PIECE, :].astype(BF)


def windows_of(own, own_rim, other, other_rim, taps):
    n, f = own.shape
    return pl.pallas_call(
        functools.partial(window_kernel, taps),
        grid=(2 * n // PIECE,),
        out_shape=jax.ShapeDtypeStruct((taps, 2 * n, f), BF),
        in_specs=[IN_VMEM] * 4,
        out_specs=pl.BlockSpec((taps, PIECE, f), lambda i: (0, i, 0)),
        scratch_shapes=[VM((2, n + 2 * RIM, f), BF), VM((PIECE + 2 * RIM, f), F32)],
        compiler_params=params(),
        cost_estimate=cost(0, 2 * (taps + 1) * 2 * n * f),
        name="windows",
    )(own, own_rim, other, other_rim)


def grad_kernel(mine_ref, got_ref, wide_ref, plus_ref, minus_ref, keep_ref, both):
    m, n = mine_ref.shape

    @pl.when(pl.program_id(0) == 0)
    def _():
        both[:, :n] = mine_ref[...]
        both[:, n:] = got_ref[...]

    total = jnp.dot(both[...], wide_ref[0], preferred_element_type=F32)
    plus_ref[0] = total[: m // 4].astype(BF)
    minus_ref[0] = total[m // 4 : m // 2].astype(BF)
    keep_ref[0] = total[m // 2 :]


def grad_parts(mine, got, wide):
    m, n = mine.shape
    taps, _, f = wide.shape
    block = lambda rows: pl.BlockSpec((1, rows, f), lambda k: (k, 0, 0))
    return pl.pallas_call(
        grad_kernel,
        grid=(taps,),
        out_shape=[
            jax.ShapeDtypeStruct((taps, m // 4, f), BF),
            jax.ShapeDtypeStruct((taps, m // 4, f), BF),
            jax.ShapeDtypeStruct((taps, m // 2, f), F32),
        ],
        in_specs=[IN_VMEM, IN_VMEM, block(2 * n)],
        out_specs=[block(m // 4), block(m // 4), block(m // 2)],
        scratch_shapes=[VM((m, 2 * n), BF)],
        compiler_params=params(),
        cost_estimate=cost(
            4 * m * n * f * taps, 2 * (2 * m * n + 2 * taps * n * f) + 3 * taps * m * f
        ),
        name="grad_parts",
    )(mine, got, wide)


def outer_rim(block, odd):
    return move(jnp.where(odd, block[-2:], block[:2]), OUTWARD)


def rim_of(odd, inner, outer):
    pad = jnp.zeros((RIM - 2, inner.shape[1]), inner.dtype)
    return jnp.concatenate(
        [pad, jnp.where(odd, inner, outer), jnp.where(odd, outer, inner), pad], axis=0
    )


EIGHTHS = ((2, 0), (1, 1), (2, 1), (3, 0), (1, 0), (3, 1), (0, 0), (0, 1))


def order_matrix(channels, seq):
    block = channels // N_SEQ
    core, x, z = seq % 2, (seq // 2) % NX, seq // (2 * NX)
    row = lax.broadcasted_iota(jnp.int32, (channels, 1), 0)
    half, eighth = row // (16 * block), (row // (2 * block)) % 8
    r1 = sum(jnp.where(eighth == e, r, 0) for e, (r, _) in enumerate(EIGHTHS))
    r2 = sum(jnp.where(eighth == e, 2 * h, 0) for e, (_, h) in enumerate(EIGHTHS))
    r2 = r2 + (row // block) % 2
    side = jnp.where(half == 0, core, 1 - core)
    to_x = (x + jnp.where(side == 0, r1, r2)) % NX
    to_z = (z + jnp.where(side == 0, r2, r1)) % NZ
    wanted = ((to_z * NX + to_x) * 2 + side) * block + row % block
    return (wanted == lax.broadcasted_iota(jnp.int32, (1, channels), 1)).astype(BF)


def ring_sums(plus, minus, keep):
    u = keep.shape[1] // 4
    wide = lambda v: v.astype(F32)
    got_p, got_m = move(plus, RINGS[0][0]), move(minus, RINGS[0][1])
    late_p = move((keep[:, :u] + wide(got_p[:, :u])).astype(BF), RINGS[0][0])
    late_m = move((keep[:, u : 2 * u] + wide(got_m[:, :u])).astype(BF), RINGS[0][1])
    low = keep[:, 2 * u : 3 * u] + wide(got_m[:, u:]) + wide(late_p)
    high = keep[:, 3 * u :] + wide(got_p[:, u:]) + wide(late_m)
    b = u // 2
    near, one, two, three = low[:, :b], low[:, b:], high[:, :b], high[:, b:]
    cut = keep.shape[0] // 2
    early = lax.broadcasted_iota(jnp.int32, near.shape, 0) < cut
    join = lambda first, last: jnp.where(early, first, last)
    got_p = move(join(two, one).astype(BF), RINGS[1][0])
    got_m = move(join(three, two).astype(BF), RINGS[1][1])
    late_p = move((one[:cut] + wide(got_p[:cut])).astype(BF), RINGS[1][0])
    late_m = move((three[cut:] + wide(got_m[cut:])).astype(BF), RINGS[1][1])
    return (
        near
        + wide(join(got_m, got_p))
        + jnp.concatenate([wide(late_p), wide(late_m)], axis=0)
    )


def body(features, conv_one, conv_two, head_vector, owner_of, donor_row, accept_row, score_grad):
    seq = lax.axis_index("seq")
    odd = seq % 2 == 1
    taps = conv_one.shape[0]
    rows_one = features.shape[0]
    rows_two = rows_one // 2
    rows_c = rows_two // 2
    records = owner_of.shape[0]
    capacity = max(2, 2 * records // N_SEQ)
    slots = N_SEQ * capacity

    feat_outer = outer_rim(features, odd)
    feat_other = move(features, SIBLING)
    feat_rim = rim_of(odd, jnp.where(odd, feat_other[-2:], feat_other[:2]), feat_outer)
    owners = owner_of
    before = (owners == owners.reshape(1, records)) & (
        lax.broadcasted_iota(jnp.int32, (records, records), 1)
        < lax.broadcasted_iota(jnp.int32, (records, records), 0)
    )
    place = owners * capacity + jnp.sum(before.astype(jnp.int32), axis=1, keepdims=True)
    placed = (place == lax.broadcasted_iota(jnp.int32, (records, slots), 1)).astype(BF)
    told = jnp.stack([donor_row.astype(BF), score_grad], 0)
    sent = jnp.dot(told, placed, preferred_element_type=F32).astype(BF)
    sent = sent.reshape(2, N_SEQ, capacity).transpose(1, 0, 2)
    heard = lax.all_to_all(sent, "seq", split_axis=0, concat_axis=0, tiled=True)
    accepts = (
        accept_row[None, :] == lax.broadcasted_iota(jnp.int32, (rows_c, records), 0)
    ).astype(BF)
    accept_pick = jnp.dot(accepts, placed, preferred_element_type=F32).astype(BF)
    accept_add = jnp.dot(
        accepts * score_grad[None, :], placed, preferred_element_type=F32
    ).astype(BF)

    order_one = order_matrix(conv_one.shape[2], seq)
    order_two = order_matrix(conv_two.shape[2], seq)

    pooled, even_one, odd_one = conv_pool(features, feat_rim, conv_one)
    pool_outer = outer_rim(pooled, odd)
    pool_other = move(pooled, SIBLING)
    pool_rim = rim_of(odd, jnp.where(odd, pool_other[-2:], pool_other[:2]), pool_outer)
    embed, even_two, odd_two = conv_pool(pooled, pool_rim, conv_two)
    feat_other_rim = rim_of(
        ~odd, jnp.where(odd, features[:2], features[-2:]), move(feat_outer, SIBLING)
    )
    pool_other_rim = rim_of(
        ~odd, jnp.where(odd, pooled[:2], pooled[-2:]), move(pool_outer, SIBLING)
    )

    heard = heard.transpose(1, 0, 2).reshape(2, slots)
    donor_hit = heard[0:1].astype(F32) == lax.broadcasted_iota(
        jnp.int32, (rows_c, slots), 0
    ).astype(F32)
    donor_pick = donor_hit.astype(BF)
    donor_add = jnp.where(donor_hit, heard[1:2], jnp.zeros((), BF))
    pick = jnp.concatenate(
        [accept_pick.reshape(rows_c, N_SEQ, capacity), donor_pick.reshape(rows_c, N_SEQ, capacity)],
        axis=2,
    ).reshape(rows_c, 2 * slots)
    add = jnp.concatenate(
        [donor_add.reshape(rows_c, N_SEQ, capacity), accept_add.reshape(rows_c, N_SEQ, capacity)],
        axis=2,
    ).reshape(rows_c, 2 * slots)
    gone = lax.dot_general(
        pick, embed, (((0,), (0,)), ((), ())), preferred_element_type=F32
    ).astype(BF)
    come = lax.all_to_all(gone, "seq", split_axis=0, concat_axis=0, tiled=True)
    own, feat_other = lax.optimization_barrier((features, feat_other, gone))[:2]
    wide_one = windows_of(own, feat_rim, feat_other, feat_other_rim, taps)
    own, pool_other = lax.optimization_barrier((pooled, pool_other, gone))[:2]
    wide_two = windows_of(own, pool_rim, pool_other, pool_other_rim, taps)

    grads, turned_two = head_back(add, come, head_vector[None, :], even_two, odd_two, order_two)
    grad_rim = rim_of(
        odd, move(jnp.where(odd, grads[:2], grads[-2:]), SIBLING), outer_rim(grads, odd)
    )
    half = turned_two.shape[0] // 2
    parts_two = grad_parts(turned_two[:half], move(turned_two[half:], SIBLING), wide_two)
    turned_one = conv_back(grads, grad_rim, conv_two, even_one, odd_one, order_one)
    half = turned_one.shape[0] // 2
    parts_one = grad_parts(turned_one[:half], move(turned_one[half:], SIBLING), wide_one)
    grad_two = ring_sums(*parts_two).transpose(1, 0, 2)
    grad_one = ring_sums(*parts_one).transpose(1, 0, 2)
    return (grad_one, grad_two)


def solution(mesh):
    in_specs = (
        P(("dp", "seq"), None),
        P(),
        P(),
        P(),
        P(("dp", "seq"), None),
        P(("dp", "seq")),
        P(("dp", "seq")),
        P(("dp", "seq")),
    )
    out_specs = (P(("dp", "seq"), None, None), P(("dp", "seq"), None, None))
    return jax.shard_map(body, mesh=mesh, in_specs=in_specs, out_specs=out_specs, check_vma=False)
```

```python
import functools

import jax
import jax.numpy as jnp
from jax import lax
from jax.experimental import pallas as pl
from jax.experimental.pallas import tpu as pltpu
from jax.sharding import PartitionSpec as P


NZ, NX = 4, 4
BF = jnp.bfloat16
F32 = jnp.float32


def index_of(z, x, c):
    return ((z % NZ) * NX + (x % NX)) * 2 + c


def pairs_of(move):
    return [
        (index_of(z, x, c), index_of(*move(z, x, c)))
        for z in range(NZ)
        for x in range(NX)
        for c in range(2)
    ]


SIBLING = pairs_of(lambda z, x, c: (z, x, 1 - c))
RINGS = (
    (
        pairs_of(lambda z, x, c: (z, x + 1, c) if c == 0 else (z + 1, x, c)),
        pairs_of(lambda z, x, c: (z, x - 1, c) if c == 0 else (z - 1, x, c)),
    ),
    (
        pairs_of(lambda z, x, c: (z + 1, x, c) if c == 0 else (z, x + 1, c)),
        pairs_of(lambda z, x, c: (z - 1, x, c) if c == 0 else (z, x - 1, c)),
    ),
)
N_SEQ = NZ * NX * 2
OUTWARD = [(s, s - 1) for s in range(2, N_SEQ, 2)] + [(s, s + 1) for s in range(1, N_SEQ - 1, 2)]


def move(value, pairs):
    return lax.ppermute(value, "seq", pairs)


VM = pltpu.VMEM
IN_VMEM = pl.BlockSpec(memory_space=pltpu.VMEM)
IN_PLACE = pl.BlockSpec(memory_space=pl.ANY)
LANES = 128
PIECE = 128
TILE = 256
RIM = 16


def params(mib=52):
    return pltpu.CompilerParams(vmem_limit_bytes=mib << 20)


def cost(flops, bytes_accessed, transcendentals=0):
    return pl.CostEstimate(
        flops=flops, bytes_accessed=bytes_accessed, transcendentals=transcendentals
    )


def gelu_both(v):
    c, a = 0.7978845608028654, 0.044715
    sq = v * v
    t = jnp.tanh(c * v * (1.0 + a * sq))
    up = 0.5 * (1.0 + t)
    return v * up, up + 0.5 * v * (1.0 - t * t) * (c * (1.0 + 3.0 * a * sq))


def fill_rims(rimmed, block_ref, rim_ref):
    n = block_ref.shape[0]
    rimmed[0:RIM] = rim_ref[0:RIM]
    rimmed[RIM : RIM + n] = block_ref[...]
    rimmed[RIM + n : 2 * RIM + n] = rim_ref[RIM : 2 * RIM]


def conv_kernel(
    taps, x_ref, rim_ref, w_hbm, pooled_ref, even_ref, odd_ref, w_ref, rimmed, piece, wide, acc, sem
):
    n, f = x_ref.shape
    copies = [
        pltpu.make_async_copy(w_hbm.at[k], w_ref.at[pl.ds(k * f, f)], sem.at[k])
        for k in range(taps)
    ]
    for copy in copies:
        copy.start()
    fill_rims(rimmed, x_ref, rim_ref)

    @pl.loop(0, n // PIECE)
    def _(m):
        r = pl.multiple_of(m * PIECE, PIECE)
        piece[...] = rimmed[pl.ds(r, PIECE + 2 * RIM), :].astype(F32)
        for k in range(taps):
            low = RIM - taps // 2 + k
            wide[pl.ds(r, PIECE), k * f : (k + 1) * f] = piece[low : low + PIECE, :].astype(BF)

    for copy in copies:
        copy.wait()

    @pl.loop(0, n // TILE)
    def _(m):
        r = pl.multiple_of(m * TILE, TILE)
        q = pl.ds(pl.multiple_of(m * (TILE // 2), TILE // 2), TILE // 2)
        total = jnp.dot(wide[pl.ds(r, TILE), :], w_ref[...], preferred_element_type=F32)
        for j in range(acc.shape[0]):
            cols = slice(j * LANES, (j + 1) * LANES)
            acc[j] = total[:, cols]
            even, even_slope = gelu_both(acc[j, pl.ds(0, TILE // 2, stride=2), :])
            odd, odd_slope = gelu_both(acc[j, pl.ds(1, TILE // 2, stride=2), :])
            pooled_ref[q, cols] = ((even + odd) * 0.5).astype(BF)
            even_ref[q, cols] = (even_slope * 0.5).astype(BF)
            odd_ref[q, cols] = (odd_slope * 0.5).astype(BF)


def conv_pool(x, rim, w):
    taps, f, c = w.shape
    n = x.shape[0]
    return pl.pallas_call(
        functools.partial(conv_kernel, taps),
        out_shape=[jax.ShapeDtypeStruct((n // 2, c), BF)]
        + [jax.ShapeDtypeStruct((n // 2, c), BF)] * 2,
        in_specs=[IN_VMEM, IN_VMEM, IN_PLACE],
        out_specs=[IN_VMEM] * 3,
        scratch_shapes=[
            VM((taps * f, c), BF),
            VM((n + 2 * RIM, f), BF),
            VM((PIECE + 2 * RIM, f), F32),
            VM((n, taps * f), BF),
            VM((c // LANES, TILE, LANES), F32),
            pltpu.SemaphoreType.DMA((taps,)),
        ],
        compiler_params=params(),
        cost_estimate=cost(2 * n * f * c * taps, 2 * (n * f + taps * f * c) + 5 * n * c, n * c),
        name="conv_pool",
    )(x, rim, w)


def back_kernel(
    taps, g_ref, rim_ref, w_hbm, even_ref, odd_ref, order_ref, out_ref, w_ref, rimmed, piece, wide, pairs, flat, sem
):
    n = g_ref.shape[0]
    copies = [pltpu.make_async_copy(w_hbm.at[k], w_ref.at[k], sem.at[k]) for k in range(taps)]
    for copy in copies:
        copy.start()
    fill_rims(rimmed, g_ref, rim_ref)

    @pl.loop(0, n // PIECE)
    def _(m):
        r = pl.multiple_of(m * PIECE, PIECE)
        piece[...] = rimmed[pl.ds(r, PIECE + 2 * RIM), :].astype(F32)
        for k in range(taps):
            low = RIM + taps // 2 - k
            wide[k, pl.ds(r, PIECE), :] = piece[low : low + PIECE, :].astype(BF)

    for copy in copies:
        copy.wait()

    @pl.loop(0, n // TILE)
    def _(m):
        r = pl.multiple_of(m * TILE, TILE)
        rows = pl.ds(r, TILE)
        total = sum(
            lax.dot_general(
                wide[k, rows, :], w_ref[k], (((1,), (1,)), ((), ())), preferred_element_type=F32
            )
            for k in range(taps)
        )
        for j in range(pairs.shape[0]):
            cols = slice(j * LANES, (j + 1) * LANES)
            pairs[j, pl.ds(0, TILE, stride=2), :] = total[:, cols] * even_ref[rows, cols]
            pairs[j, pl.ds(1, TILE, stride=2), :] = total[:, cols] * odd_ref[rows, cols]
            flat[:, cols] = pairs[j].astype(BF)
        turned = lax.dot_general(
            order_ref[...], flat[...], (((1,), (1,)), ((), ())), preferred_element_type=F32
        )
        out_ref[:, pl.ds(pl.multiple_of(2 * r, 2 * TILE), 2 * TILE)] = turned.astype(BF)


def conv_back(g, rim, w, even, odd, order):
    taps, f, c = w.shape
    n = g.shape[0]
    return pl.pallas_call(
        functools.partial(back_kernel, taps),
        out_shape=jax.ShapeDtypeStruct((f, 2 * n), BF),
        in_specs=[IN_VMEM, IN_VMEM, IN_PLACE, IN_VMEM, IN_VMEM, IN_VMEM],
        out_specs=IN_VMEM,
        scratch_shapes=[
            VM((taps, f, c), BF),
            VM((n + 2 * RIM, c), BF),
            VM((PIECE + 2 * RIM, c), F32),
            VM((taps, n, c), BF),
            VM((f // LANES, 2 * TILE, LANES), F32),
            VM((2 * TILE, f), BF),
            pltpu.SemaphoreType.DMA((taps,)),
        ],
        compiler_params=params(),
        cost_estimate=cost(
            2 * n * f * c * taps + 4 * n * f * f, 2 * (n * c + taps * f * c + f * f) + 12 * n * f
        ),
        name="conv_back",
    )(g, rim, w, even, odd, order)


def head_kernel(add_ref, come_ref, head_ref, even_ref, odd_ref, order_ref, g_ref, turned_ref, pairs):
    n = add_ref.shape[0]
    total = jnp.dot(add_ref[...], come_ref[...], preferred_element_type=F32) * head_ref[...]
    for j in range(pairs.shape[0]):
        cols = slice(j * LANES, (j + 1) * LANES)
        pairs[j, pl.ds(0, n, stride=2), :] = total[:, cols] * even_ref[:, cols]
        pairs[j, pl.ds(1, n, stride=2), :] = total[:, cols] * odd_ref[:, cols]
        g_ref[:, cols] = pairs[j].astype(BF)
    turned_ref[...] = lax.dot_general(
        order_ref[...], g_ref[...], (((1,), (1,)), ((), ())), preferred_element_type=F32
    ).astype(BF)


def head_back(add, come, head, even, odd, order):
    n, c = even.shape
    return pl.pallas_call(
        head_kernel,
        out_shape=[jax.ShapeDtypeStruct((2 * n, c), BF), jax.ShapeDtypeStruct((c, 2 * n), BF)],
        in_specs=[IN_VMEM] * 6,
        out_specs=[IN_VMEM] * 2,
        scratch_shapes=[VM((c // LANES, 2 * n, LANES), F32)],
        compiler_params=params(),
        cost_estimate=cost(
            2 * n * c * come.shape[0] + 4 * n * c * c, 2 * (come.size + add.size + c * c) + 16 * n * c
        ),
        name="head_back",
    )(add, come, head, even, odd, order)


def window_kernel(taps, own_ref, own_rim, other_ref, other_rim, out_ref, rimmed, piece):
    n = own_ref.shape[0]
    step = pl.program_id(0)

    @pl.when(step == 0)
    def _():
        fill_rims(rimmed.at[0], own_ref, own_rim)
        fill_rims(rimmed.at[1], other_ref, other_rim)

    per = n // PIECE
    side, m = step // per, step % per
    r = pl.multiple_of(m * PIECE, PIECE)
    piece[...] = rimmed[side, pl.ds(r, PIECE + 2 * RIM), :].astype(F32)
    for k in range(taps):
        low = RIM - taps // 2 + k
        out_ref[k] = piece[low : low + PIECE, :].astype(BF)


def windows_of(own, own_rim, other, other_rim, taps):
    n, f = own.shape
    return pl.pallas_call(
        functools.partial(window_kernel, taps),
        grid=(2 * n // PIECE,),
        out_shape=pltpu.HBM((taps, 2 * n, f), BF),
        in_specs=[IN_VMEM] * 4,
        out_specs=pl.BlockSpec((taps, PIECE, f), lambda i: (0, i, 0)),
        scratch_shapes=[VM((2, n + 2 * RIM, f), BF), VM((PIECE + 2 * RIM, f), F32)],
        compiler_params=params(),
        cost_estimate=cost(0, 2 * (taps + 1) * 2 * n * f),
        name="windows",
    )(own, own_rim, other, other_rim)


def grad_kernel(mine_ref, got_ref, wide_ref, plus_ref, minus_ref, keep_ref, both):
    m, n = mine_ref.shape

    @pl.when(pl.program_id(0) == 0)
    def _():
        both[:, :n] = mine_ref[...]
        both[:, n:] = got_ref[...]

    total = jnp.dot(both[...], wide_ref[0], preferred_element_type=F32)
    plus_ref[0] = total[: m // 4].astype(BF)
    minus_ref[0] = total[m // 4 : m // 2].astype(BF)
    keep_ref[0] = total[m // 2 :]


def grad_parts(mine, got, wide):
    m, n = mine.shape
    taps, _, f = wide.shape
    block = lambda rows: pl.BlockSpec((1, rows, f), lambda k: (k, 0, 0))
    return pl.pallas_call(
        grad_kernel,
        grid=(taps,),
        out_shape=[
            pltpu.HBM((taps, m // 4, f), BF),
            pltpu.HBM((taps, m // 4, f), BF),
            pltpu.HBM((taps, m // 2, f), F32),
        ],
        in_specs=[IN_VMEM, IN_VMEM, block(2 * n)],
        out_specs=[block(m // 4), block(m // 4), block(m // 2)],
        scratch_shapes=[VM((m, 2 * n), BF)],
        compiler_params=params(),
        cost_estimate=cost(
            4 * m * n * f * taps, 2 * (2 * m * n + 2 * taps * n * f) + 3 * taps * m * f
        ),
        name="grad_parts",
    )(mine, got, wide)


def outer_rim(block, odd):
    return move(jnp.where(odd, block[-2:], block[:2]), OUTWARD)


def rim_of(odd, inner, outer):
    pad = jnp.zeros((RIM - 2, inner.shape[1]), inner.dtype)
    return jnp.concatenate(
        [pad, jnp.where(odd, inner, outer), jnp.where(odd, outer, inner), pad], axis=0
    )


EIGHTHS = ((2, 0), (1, 1), (2, 1), (3, 0), (1, 0), (3, 1), (0, 0), (0, 1))


def order_matrix(channels, seq):
    block = channels // N_SEQ
    core, x, z = seq % 2, (seq // 2) % NX, seq // (2 * NX)
    row = lax.broadcasted_iota(jnp.int32, (channels, 1), 0)
    half, eighth = row // (16 * block), (row // (2 * block)) % 8
    r1 = sum(jnp.where(eighth == e, r, 0) for e, (r, _) in enumerate(EIGHTHS))
    r2 = sum(jnp.where(eighth == e, 2 * h, 0) for e, (_, h) in enumerate(EIGHTHS))
    r2 = r2 + (row // block) % 2
    side = jnp.where(half == 0, core, 1 - core)
    to_x = (x + jnp.where(side == 0, r1, r2)) % NX
    to_z = (z + jnp.where(side == 0, r2, r1)) % NZ
    wanted = ((to_z * NX + to_x) * 2 + side) * block + row % block
    return (wanted == lax.broadcasted_iota(jnp.int32, (1, channels), 1)).astype(BF)


def ring_sums(plus, minus, keep):
    u = keep.shape[1] // 4
    wide = lambda v: v.astype(F32)
    got_p = move(plus, RINGS[0][0])
    got_m = move(minus, RINGS[0][1])
    late_p = move((keep[:, :u] + wide(got_p[:, :u])).astype(BF), RINGS[0][0])
    late_m = move((keep[:, u : 2 * u] + wide(got_m[:, :u])).astype(BF), RINGS[0][1])
    low = keep[:, 2 * u : 3 * u] + wide(got_m[:, u:]) + wide(late_p)
    high = keep[:, 3 * u :] + wide(got_p[:, u:]) + wide(late_m)
    b = u // 2
    near, one, two, three = low[:, :b], low[:, b:], high[:, :b], high[:, b:]
    cut = keep.shape[0] // 2
    early = lax.broadcasted_iota(jnp.int32, near.shape, 0) < cut
    join = lambda first, last: jnp.where(early, first, last)
    got_p = move(join(two, one).astype(BF), RINGS[1][0])
    got_m = move(join(three, two).astype(BF), RINGS[1][1])
    late_p = move((one[:cut] + wide(got_p[:cut])).astype(BF), RINGS[1][0])
    late_m = move((three[cut:] + wide(got_m[cut:])).astype(BF), RINGS[1][1])
    return (
        near
        + wide(join(got_m, got_p))
        + jnp.concatenate([wide(late_p), wide(late_m)], axis=0)
    )


def body(features, conv_one, conv_two, head_vector, owner_of, donor_row, accept_row, score_grad):
    seq = lax.axis_index("seq")
    odd = seq % 2 == 1
    taps = conv_one.shape[0]
    rows_one = features.shape[0]
    rows_two = rows_one // 2
    rows_c = rows_two // 2
    records = owner_of.shape[0]
    capacity = max(2, 2 * records // N_SEQ)
    slots = N_SEQ * capacity

    feat_outer = outer_rim(features, odd)
    feat_other = move(features, SIBLING)
    feat_rim = rim_of(odd, jnp.where(odd, feat_other[-2:], feat_other[:2]), feat_outer)
    owners = owner_of
    before = (owners == owners.reshape(1, records)) & (
        lax.broadcasted_iota(jnp.int32, (records, records), 1)
        < lax.broadcasted_iota(jnp.int32, (records, records), 0)
    )
    place = owners * capacity + jnp.sum(before.astype(jnp.int32), axis=1, keepdims=True)
    placed = (place == lax.broadcasted_iota(jnp.int32, (records, slots), 1)).astype(BF)
    told = jnp.stack([donor_row.astype(BF), score_grad], 0)
    sent = jnp.dot(told, placed, preferred_element_type=F32).astype(BF)
    sent = sent.reshape(2, N_SEQ, capacity).transpose(1, 0, 2)
    heard = lax.all_to_all(sent, "seq", split_axis=0, concat_axis=0, tiled=True)
    accepts = (
        accept_row[None, :] == lax.broadcasted_iota(jnp.int32, (rows_c, records), 0)
    ).astype(BF)
    accept_pick = jnp.dot(accepts, placed, preferred_element_type=F32).astype(BF)
    accept_add = jnp.dot(
        accepts * score_grad[None, :], placed, preferred_element_type=F32
    ).astype(BF)

    order_one = order_matrix(conv_one.shape[2], seq)
    order_two = order_matrix(conv_two.shape[2], seq)

    pooled, even_one, odd_one = conv_pool(features, feat_rim, conv_one)
    pool_outer = outer_rim(pooled, odd)
    pool_other = move(pooled, SIBLING)
    pool_rim = rim_of(odd, jnp.where(odd, pool_other[-2:], pool_other[:2]), pool_outer)
    embed, even_two, odd_two = conv_pool(pooled, pool_rim, conv_two)
    feat_other_rim = rim_of(
        ~odd, jnp.where(odd, features[:2], features[-2:]), move(feat_outer, SIBLING)
    )
    pool_other_rim = rim_of(
        ~odd, jnp.where(odd, pooled[:2], pooled[-2:]), move(pool_outer, SIBLING)
    )

    heard = lax.optimization_barrier((heard, pooled))[0]
    heard = heard.transpose(1, 0, 2).reshape(2, slots)
    donor_hit = heard[0:1].astype(F32) == lax.broadcasted_iota(
        jnp.int32, (rows_c, slots), 0
    ).astype(F32)
    donor_pick = donor_hit.astype(BF)
    donor_add = jnp.where(donor_hit, heard[1:2], jnp.zeros((), BF))
    pick = jnp.concatenate(
        [accept_pick.reshape(rows_c, N_SEQ, capacity), donor_pick.reshape(rows_c, N_SEQ, capacity)],
        axis=2,
    ).reshape(rows_c, 2 * slots)
    add = jnp.concatenate(
        [donor_add.reshape(rows_c, N_SEQ, capacity), accept_add.reshape(rows_c, N_SEQ, capacity)],
        axis=2,
    ).reshape(rows_c, 2 * slots)
    gone = lax.dot_general(
        pick, embed, (((0,), (0,)), ((), ())), preferred_element_type=F32
    ).astype(BF)
    come = lax.all_to_all(gone, "seq", split_axis=0, concat_axis=0, tiled=True)
    own, feat_other = lax.optimization_barrier((features, feat_other, gone))[:2]
    wide_one = windows_of(own, feat_rim, feat_other, feat_other_rim, taps)
    own, pool_other = lax.optimization_barrier((pooled, pool_other, gone))[:2]
    wide_two = windows_of(own, pool_rim, pool_other, pool_other_rim, taps)

    come, wide_one, wide_two = lax.optimization_barrier((come, wide_one, wide_two))
    grads, turned_two = head_back(add, come, head_vector[None, :], even_two, odd_two, order_two)
    grad_rim = rim_of(
        odd, move(jnp.where(odd, grads[:2], grads[-2:]), SIBLING), outer_rim(grads, odd)
    )
    half = turned_two.shape[0] // 2
    parts_two = grad_parts(turned_two[:half], move(turned_two[half:], SIBLING), wide_two)
    grads = lax.optimization_barrier((grads, parts_two))[0]
    turned_one = conv_back(grads, grad_rim, conv_two, even_one, odd_one, order_one)
    half = turned_one.shape[0] // 2
    got = move(turned_one[half:], SIBLING)
    parts_one = grad_parts(turned_one[:half], got, wide_one)
    grad_two = ring_sums(*parts_two).transpose(1, 0, 2)
    grad_one = ring_sums(*parts_one).transpose(1, 0, 2)
    return (grad_one, grad_two)


def solution(mesh):
    in_specs = (
        P(("dp", "seq"), None),
        P(),
        P(),
        P(),
        P(("dp", "seq"), None),
        P(("dp", "seq")),
        P(("dp", "seq")),
        P(("dp", "seq")),
    )
    out_specs = (P(("dp", "seq"), None, None), P(("dp", "seq"), None, None))

    return jax.shard_map(body, mesh=mesh, in_specs=in_specs, out_specs=out_specs, check_vma=False)
```

```python
import functools

import jax
import jax.numpy as jnp
from jax import lax
from jax.experimental import pallas as pl
from jax.experimental.pallas import tpu as pltpu
from jax.sharding import PartitionSpec as P


NZ, NX = 4, 4
BF = jnp.bfloat16
F32 = jnp.float32


def index_of(z, x, c):
    return ((z % NZ) * NX + (x % NX)) * 2 + c


def pairs_of(move):
    return [
        (index_of(z, x, c), index_of(*move(z, x, c)))
        for z in range(NZ)
        for x in range(NX)
        for c in range(2)
    ]


SIBLING = pairs_of(lambda z, x, c: (z, x, 1 - c))
RINGS = (
    (
        pairs_of(lambda z, x, c: (z, x + 1, c) if c == 0 else (z + 1, x, c)),
        pairs_of(lambda z, x, c: (z, x - 1, c) if c == 0 else (z - 1, x, c)),
    ),
    (
        pairs_of(lambda z, x, c: (z + 1, x, c) if c == 0 else (z, x + 1, c)),
        pairs_of(lambda z, x, c: (z - 1, x, c) if c == 0 else (z, x - 1, c)),
    ),
)
N_SEQ = NZ * NX * 2
OUTWARD = [(s, s - 1) for s in range(2, N_SEQ, 2)] + [(s, s + 1) for s in range(1, N_SEQ - 1, 2)]


def move(value, pairs):
    return lax.ppermute(value, "seq", pairs)


VM = pltpu.VMEM
IN_VMEM = pl.BlockSpec(memory_space=pltpu.VMEM)
IN_PLACE = pl.BlockSpec(memory_space=pl.ANY)
LANES = 128
PIECE = 128
TILE = 256
RIM = 16


def params(mib=44):
    return pltpu.CompilerParams(vmem_limit_bytes=mib << 20)


def cost(flops, bytes_accessed, transcendentals=0):
    return pl.CostEstimate(
        flops=flops, bytes_accessed=bytes_accessed, transcendentals=transcendentals
    )


def gelu_both(v):
    c, a = 0.7978845608028654, 0.044715
    sq = v * v
    t = jnp.tanh(c * v * (1.0 + a * sq))
    up = 0.5 * (1.0 + t)
    return v * up, up + 0.5 * v * (1.0 - t * t) * (c * (1.0 + 3.0 * a * sq))


def fill_rims(rimmed, block_ref, rim_ref):
    n = block_ref.shape[0]
    rimmed[0:RIM] = rim_ref[0:RIM]
    rimmed[RIM : RIM + n] = block_ref[...]
    rimmed[RIM + n : 2 * RIM + n] = rim_ref[RIM : 2 * RIM]


def conv_kernel(
    taps, x_ref, rim_ref, w_hbm, pooled_ref, even_ref, odd_ref, w_ref, rimmed, piece, wide, acc, sem
):
    n, f = x_ref.shape
    copies = [
        pltpu.make_async_copy(w_hbm.at[k], w_ref.at[pl.ds(k * f, f)], sem.at[k])
        for k in range(taps)
    ]
    for copy in copies:
        copy.start()
    fill_rims(rimmed, x_ref, rim_ref)

    @pl.loop(0, n // PIECE)
    def _(m):
        r = pl.multiple_of(m * PIECE, PIECE)
        piece[...] = rimmed[pl.ds(r, PIECE + 2 * RIM), :].astype(F32)
        for k in range(taps):
            low = RIM - taps // 2 + k
            wide[pl.ds(r, PIECE), k * f : (k + 1) * f] = piece[low : low + PIECE, :].astype(BF)

    for copy in copies:
        copy.wait()

    @pl.loop(0, n // TILE)
    def _(m):
        r = pl.multiple_of(m * TILE, TILE)
        q = pl.ds(pl.multiple_of(m * (TILE // 2), TILE // 2), TILE // 2)
        total = jnp.dot(wide[pl.ds(r, TILE), :], w_ref[...], preferred_element_type=F32)
        for j in range(acc.shape[0]):
            cols = slice(j * LANES, (j + 1) * LANES)
            acc[j] = total[:, cols]
            even, even_slope = gelu_both(acc[j, pl.ds(0, TILE // 2, stride=2), :])
            odd, odd_slope = gelu_both(acc[j, pl.ds(1, TILE // 2, stride=2), :])
            pooled_ref[q, cols] = ((even + odd) * 0.5).astype(BF)
            even_ref[q, cols] = even_slope * 0.5
            odd_ref[q, cols] = odd_slope * 0.5


def conv_pool(x, rim, w):
    taps, f, c = w.shape
    n = x.shape[0]
    return pl.pallas_call(
        functools.partial(conv_kernel, taps),
        out_shape=[jax.ShapeDtypeStruct((n // 2, c), BF)]
        + [jax.ShapeDtypeStruct((n // 2, c), F32)] * 2,
        in_specs=[IN_VMEM, IN_VMEM, IN_PLACE],
        out_specs=[IN_VMEM] * 3,
        scratch_shapes=[
            VM((taps * f, c), BF),
            VM((n + 2 * RIM, f), BF),
            VM((PIECE + 2 * RIM, f), F32),
            VM((n, taps * f), BF),
            VM((c // LANES, TILE, LANES), F32),
            pltpu.SemaphoreType.DMA((taps,)),
        ],
        compiler_params=params(),
        cost_estimate=cost(2 * n * f * c * taps, 2 * (n * f + taps * f * c) + 5 * n * c, n * c),
        name="conv_pool",
    )(x, rim, w)


def back_kernel(
    taps, g_ref, rim_ref, w_hbm, even_ref, odd_ref, order_ref, mine_ref, theirs_ref, w_ref, rimmed, piece, wide, pairs, flat, sem
):
    n = g_ref.shape[0]
    copies = [pltpu.make_async_copy(w_hbm.at[k], w_ref.at[k], sem.at[k]) for k in range(taps)]
    for copy in copies:
        copy.start()
    fill_rims(rimmed, g_ref, rim_ref)

    @pl.loop(0, n // PIECE)
    def _(m):
        r = pl.multiple_of(m * PIECE, PIECE)
        piece[...] = rimmed[pl.ds(r, PIECE + 2 * RIM), :].astype(F32)
        for k in range(taps):
            low = RIM + taps // 2 - k
            wide[k, pl.ds(r, PIECE), :] = piece[low : low + PIECE, :].astype(BF)

    for copy in copies:
        copy.wait()

    @pl.loop(0, n // TILE)
    def _(m):
        r = pl.multiple_of(m * TILE, TILE)
        rows = pl.ds(r, TILE)
        total = sum(
            lax.dot_general(
                wide[k, rows, :], w_ref[k], (((1,), (1,)), ((), ())), preferred_element_type=F32
            )
            for k in range(taps)
        )
        for j in range(pairs.shape[0]):
            cols = slice(j * LANES, (j + 1) * LANES)
            pairs[j, pl.ds(0, TILE, stride=2), :] = total[:, cols] * even_ref[rows, cols]
            pairs[j, pl.ds(1, TILE, stride=2), :] = total[:, cols] * odd_ref[rows, cols]
            flat[:, cols] = pairs[j].astype(BF)
        turned = lax.dot_general(
            order_ref[...], flat[...], (((1,), (1,)), ((), ())), preferred_element_type=F32
        )
        half = mine_ref.shape[0]
        cols = pl.ds(pl.multiple_of(2 * r, 2 * TILE), 2 * TILE)
        mine_ref[:, cols] = turned[:half].astype(BF)
        theirs_ref[:, cols] = turned[half:].astype(BF)


def conv_back(g, rim, w, even, odd, order):
    taps, f, c = w.shape
    n = g.shape[0]
    return pl.pallas_call(
        functools.partial(back_kernel, taps),
        out_shape=[jax.ShapeDtypeStruct((f // 2, 2 * n), BF)] * 2,
        in_specs=[IN_VMEM, IN_VMEM, IN_PLACE, IN_VMEM, IN_VMEM, IN_VMEM],
        out_specs=[IN_VMEM] * 2,
        scratch_shapes=[
            VM((taps, f, c), BF),
            VM((n + 2 * RIM, c), BF),
            VM((PIECE + 2 * RIM, c), F32),
            VM((taps, n, c), BF),
            VM((f // LANES, 2 * TILE, LANES), F32),
            VM((2 * TILE, f), BF),
            pltpu.SemaphoreType.DMA((taps,)),
        ],
        compiler_params=params(),
        cost_estimate=cost(
            2 * n * f * c * taps + 4 * n * f * f, 2 * (n * c + taps * f * c + f * f) + 12 * n * f
        ),
        name="conv_back",
    )(g, rim, w, even, odd, order)


def head_kernel(add_ref, come_ref, head_ref, even_ref, odd_ref, order_ref, g_ref, mine_ref, theirs_ref, pairs):
    n = add_ref.shape[0]
    total = jnp.dot(add_ref[...], come_ref[...], preferred_element_type=F32) * head_ref[...]
    for j in range(pairs.shape[0]):
        cols = slice(j * LANES, (j + 1) * LANES)
        pairs[j, pl.ds(0, n, stride=2), :] = total[:, cols] * even_ref[:, cols]
        pairs[j, pl.ds(1, n, stride=2), :] = total[:, cols] * odd_ref[:, cols]
        g_ref[:, cols] = pairs[j].astype(BF)
    turned = lax.dot_general(
        order_ref[...], g_ref[...], (((1,), (1,)), ((), ())), preferred_element_type=F32
    )
    half = mine_ref.shape[0]
    mine_ref[...] = turned[:half].astype(BF)
    theirs_ref[...] = turned[half:].astype(BF)


def head_back(add, come, head, even, odd, order):
    n, c = even.shape
    return pl.pallas_call(
        head_kernel,
        out_shape=[jax.ShapeDtypeStruct((2 * n, c), BF)]
        + [jax.ShapeDtypeStruct((c // 2, 2 * n), BF)] * 2,
        in_specs=[IN_VMEM] * 6,
        out_specs=[IN_VMEM] * 3,
        scratch_shapes=[VM((c // LANES, 2 * n, LANES), F32)],
        compiler_params=params(),
        cost_estimate=cost(
            2 * n * c * come.shape[0] + 4 * n * c * c, 2 * (come.size + add.size + c * c) + 16 * n * c
        ),
        name="head_back",
    )(add, come, head, even, odd, order)


def window_kernel(taps, own_ref, own_rim, other_ref, other_rim, out_ref, rimmed, piece):
    n = own_ref.shape[0]
    step = pl.program_id(0)

    @pl.when(step == 0)
    def _():
        fill_rims(rimmed.at[0], own_ref, own_rim)
        fill_rims(rimmed.at[1], other_ref, other_rim)

    per = n // PIECE
    side, m = step // per, step % per
    r = pl.multiple_of(m * PIECE, PIECE)
    piece[...] = rimmed[side, pl.ds(r, PIECE + 2 * RIM), :].astype(F32)
    for k in range(taps):
        low = RIM - taps // 2 + k
        out_ref[k] = piece[low : low + PIECE, :].astype(BF)


def windows_of(own, own_rim, other, other_rim, taps):
    n, f = own.shape
    return pl.pallas_call(
        functools.partial(window_kernel, taps),
        grid=(2 * n // PIECE,),
        out_shape=pltpu.HBM((taps, 2 * n, f), BF),
        in_specs=[IN_VMEM] * 4,
        out_specs=pl.BlockSpec((taps, PIECE, f), lambda i: (0, i, 0)),
        scratch_shapes=[VM((2, n + 2 * RIM, f), BF), VM((PIECE + 2 * RIM, f), F32)],
        compiler_params=params(),
        cost_estimate=cost(0, 2 * (taps + 1) * 2 * n * f),
        name="windows",
    )(own, own_rim, other, other_rim)


def grad_kernel(mine_ref, got_ref, wide_ref, plus_ref, minus_ref, keep_ref, both):
    m, n = mine_ref.shape

    @pl.when(pl.program_id(0) == 0)
    def _():
        both[:, :n] = mine_ref[...]
        both[:, n:] = got_ref[...]

    total = jnp.dot(both[...], wide_ref[0], preferred_element_type=F32)
    plus_ref[0] = total[: m // 4].astype(BF)
    minus_ref[0] = total[m // 4 : m // 2].astype(BF)
    keep_ref[0] = total[m // 2 :]


def grad_parts(mine, got, wide):
    m, n = mine.shape
    taps, _, f = wide.shape
    block = lambda rows: pl.BlockSpec((1, rows, f), lambda k: (k, 0, 0))
    return pl.pallas_call(
        grad_kernel,
        grid=(taps,),
        out_shape=[
            pltpu.HBM((taps, m // 4, f), BF),
            pltpu.HBM((taps, m // 4, f), BF),
            pltpu.HBM((taps, m // 2, f), F32),
        ],
        in_specs=[IN_VMEM, IN_VMEM, block(2 * n)],
        out_specs=[block(m // 4), block(m // 4), block(m // 2)],
        scratch_shapes=[VM((m, 2 * n), BF)],
        compiler_params=params(),
        cost_estimate=cost(
            4 * m * n * f * taps, 2 * (2 * m * n + 2 * taps * n * f) + 3 * taps * m * f
        ),
        name="grad_parts",
    )(mine, got, pltpu.with_memory_space_constraint(wide, pltpu.HBM))


def outer_rim(block, odd):
    return move(jnp.where(odd, block[-2:], block[:2]), OUTWARD)


def rim_of(odd, inner, outer):
    pad = jnp.zeros((RIM - 2, inner.shape[1]), inner.dtype)
    return jnp.concatenate(
        [pad, jnp.where(odd, inner, outer), jnp.where(odd, outer, inner), pad], axis=0
    )


EIGHTHS = ((2, 0), (1, 1), (2, 1), (3, 0), (1, 0), (3, 1), (0, 0), (0, 1))


def order_matrix(channels, seq):
    block = channels // N_SEQ
    core, x, z = seq % 2, (seq // 2) % NX, seq // (2 * NX)
    row = lax.broadcasted_iota(jnp.int32, (channels, 1), 0)
    half, eighth = row // (16 * block), (row // (2 * block)) % 8
    r1 = sum(jnp.where(eighth == e, r, 0) for e, (r, _) in enumerate(EIGHTHS))
    r2 = sum(jnp.where(eighth == e, 2 * h, 0) for e, (_, h) in enumerate(EIGHTHS))
    r2 = r2 + (row // block) % 2
    side = jnp.where(half == 0, core, 1 - core)
    to_x = (x + jnp.where(side == 0, r1, r2)) % NX
    to_z = (z + jnp.where(side == 0, r2, r1)) % NZ
    wanted = ((to_z * NX + to_x) * 2 + side) * block + row % block
    return (wanted == lax.broadcasted_iota(jnp.int32, (1, channels), 1)).astype(BF)


def ring_sums(plus, minus, keep):
    u = keep.shape[1] // 4
    wide = lambda v: v.astype(F32)
    got_p = move(plus, RINGS[0][0])
    got_m = move(minus, RINGS[0][1])
    on_p, on_m = lax.optimization_barrier(
        (
            (keep[:, :u] + wide(got_p[:, :u])).astype(BF),
            (keep[:, u : 2 * u] + wide(got_m[:, :u])).astype(BF),
        )
    )
    late_p = move(on_p, RINGS[0][0])
    late_m = move(on_m, RINGS[0][1])
    low = keep[:, 2 * u : 3 * u] + wide(got_m[:, u:]) + wide(late_p)
    high = keep[:, 3 * u :] + wide(got_p[:, u:]) + wide(late_m)
    b = u // 2
    near, one, two, three = low[:, :b], low[:, b:], high[:, :b], high[:, b:]
    cut = keep.shape[0] // 2
    early = lax.broadcasted_iota(jnp.int32, near.shape, 0) < cut
    join = lambda first, last: jnp.where(early, first, last)
    on_p, on_m = lax.optimization_barrier(
        (join(two, one).astype(BF), join(three, two).astype(BF))
    )
    got_p, got_m = move(on_p, RINGS[1][0]), move(on_m, RINGS[1][1])
    on_p, on_m = lax.optimization_barrier(
        (
            (one[:cut] + wide(got_p[:cut])).astype(BF),
            (three[cut:] + wide(got_m[cut:])).astype(BF),
        )
    )
    late_p, late_m = move(on_p, RINGS[1][0]), move(on_m, RINGS[1][1])
    return (
        near
        + wide(join(got_m, got_p))
        + jnp.concatenate([wide(late_p), wide(late_m)], axis=0)
    )


def body(features, conv_one, conv_two, head_vector, owner_of, donor_row, accept_row, score_grad):
    seq = lax.axis_index("seq")
    odd = seq % 2 == 1
    taps = conv_one.shape[0]
    rows_one = features.shape[0]
    rows_two = rows_one // 2
    rows_c = rows_two // 2
    records = owner_of.shape[0]
    capacity = max(2, 2 * records // N_SEQ)
    slots = N_SEQ * capacity

    feat_outer = outer_rim(features, odd)
    feat_other = move(features, SIBLING)
    feat_rim = rim_of(odd, jnp.where(odd, feat_other[-2:], feat_other[:2]), feat_outer)
    owners = owner_of
    before = (owners == owners.reshape(1, records)) & (
        lax.broadcasted_iota(jnp.int32, (records, records), 1)
        < lax.broadcasted_iota(jnp.int32, (records, records), 0)
    )
    place = owners * capacity + jnp.sum(before.astype(jnp.int32), axis=1, keepdims=True)
    placed = (place == lax.broadcasted_iota(jnp.int32, (records, slots), 1)).astype(BF)
    told = jnp.stack([donor_row.astype(BF), score_grad], 0)
    sent = jnp.dot(told, placed, preferred_element_type=F32).astype(BF)
    sent = sent.reshape(2, N_SEQ, capacity).transpose(1, 0, 2)
    heard = lax.all_to_all(sent, "seq", split_axis=0, concat_axis=0, tiled=True)
    accepts = (
        accept_row[None, :] == lax.broadcasted_iota(jnp.int32, (rows_c, records), 0)
    ).astype(BF)
    accept_pick = jnp.dot(accepts, placed, preferred_element_type=F32).astype(BF)
    accept_add = jnp.dot(
        accepts * score_grad[None, :], placed, preferred_element_type=F32
    ).astype(BF)

    order_one = order_matrix(conv_one.shape[2], seq)
    order_two = order_matrix(conv_two.shape[2], seq)

    pooled, even_one, odd_one = conv_pool(features, feat_rim, conv_one)
    pool_outer = outer_rim(pooled, odd)
    pool_other = move(pooled, SIBLING)
    pool_rim = rim_of(odd, jnp.where(odd, pool_other[-2:], pool_other[:2]), pool_outer)
    embed, even_two, odd_two = conv_pool(pooled, pool_rim, conv_two)
    heard = lax.optimization_barrier((heard, pooled))[0]
    heard = heard.transpose(1, 0, 2).reshape(2, slots)
    donor_hit = heard[0:1].astype(F32) == lax.broadcasted_iota(
        jnp.int32, (rows_c, slots), 0
    ).astype(F32)
    donor_pick = donor_hit.astype(BF)
    donor_add = jnp.where(donor_hit, heard[1:2], jnp.zeros((), BF))
    pick = jnp.concatenate(
        [accept_pick.reshape(rows_c, N_SEQ, capacity), donor_pick.reshape(rows_c, N_SEQ, capacity)],
        axis=2,
    ).reshape(rows_c, 2 * slots)
    add = jnp.concatenate(
        [donor_add.reshape(rows_c, N_SEQ, capacity), accept_add.reshape(rows_c, N_SEQ, capacity)],
        axis=2,
    ).reshape(rows_c, 2 * slots)
    gone = lax.dot_general(
        pick, embed, (((0,), (0,)), ((), ())), preferred_element_type=F32
    ).astype(BF)
    come = lax.all_to_all(gone, "seq", split_axis=0, concat_axis=0, tiled=True)
    own, feat_other, outer, pool, pool_other, outer_two, _ = lax.optimization_barrier(
        (features, feat_other, feat_outer, pooled, pool_other, pool_outer, gone)
    )
    rim = rim_of(~odd, jnp.where(odd, own[:2], own[-2:]), move(outer, SIBLING))
    wide_one = windows_of(own, feat_rim, feat_other, rim, taps)
    rim = rim_of(~odd, jnp.where(odd, pool[:2], pool[-2:]), move(outer_two, SIBLING))
    wide_two = windows_of(pool, pool_rim, pool_other, rim, taps)
    come, wide_one, wide_two, order_one, order_two, add = lax.optimization_barrier(
        (come, wide_one, wide_two, order_one, order_two, add)
    )
    grads, mine_two, theirs_two = head_back(add, come, head_vector[None, :], even_two, odd_two, order_two)
    grad_rim = rim_of(
        odd, move(jnp.where(odd, grads[:2], grads[-2:]), SIBLING), outer_rim(grads, odd)
    )
    parts_two = grad_parts(mine_two, move(theirs_two, SIBLING), wide_two)
    grads = lax.optimization_barrier((grads, parts_two))[0]
    mine_one, theirs_one = conv_back(
        grads, grad_rim, conv_two, even_one, odd_one, order_one
    )
    got = move(theirs_one, SIBLING)
    parts_one = grad_parts(mine_one, got, wide_one)
    grad_two = ring_sums(*parts_two).transpose(1, 0, 2)
    grad_one = ring_sums(*parts_one).transpose(1, 0, 2)
    return (grad_one, grad_two)


def solution(mesh):
    in_specs = (
        P(("dp", "seq"), None),
        P(),
        P(),
        P(),
        P(("dp", "seq"), None),
        P(("dp", "seq")),
        P(("dp", "seq")),
        P(("dp", "seq")),
    )
    out_specs = (P(("dp", "seq"), None, None), P(("dp", "seq"), None, None))

    return jax.shard_map(body, mesh=mesh, in_specs=in_specs, out_specs=out_specs, check_vma=False)
```

```python
import functools

import jax
import jax.numpy as jnp
from jax import lax
from jax.experimental import pallas as pl
from jax.experimental.pallas import tpu as pltpu
from jax.sharding import PartitionSpec as P


NZ, NX = 4, 4
BF = jnp.bfloat16
F32 = jnp.float32


def index_of(z, x, c):
    return ((z % NZ) * NX + (x % NX)) * 2 + c


def pairs_of(move):
    return [
        (index_of(z, x, c), index_of(*move(z, x, c)))
        for z in range(NZ)
        for x in range(NX)
        for c in range(2)
    ]


SIBLING = pairs_of(lambda z, x, c: (z, x, 1 - c))
WAYS = tuple(
    tuple(
        pairs_of(lambda z, x, c: (z, x + r, c) if c == first else (z + r, x, c)) for r in (1, 2, 3)
    )
    for first in (0, 1)
)
N_SEQ = NZ * NX * 2
OUTWARD = [(s, s - 1) for s in range(2, N_SEQ, 2)] + [(s, s + 1) for s in range(1, N_SEQ - 1, 2)]


def move(value, pairs):
    return lax.ppermute(value, "seq", pairs)


VM = pltpu.VMEM
IN_VMEM = pl.BlockSpec(memory_space=pltpu.VMEM)
IN_PLACE = pl.BlockSpec(memory_space=pl.ANY)
LANES = 128
PIECE = 128
TILE = 256
RIM = 16


def in_hbm(value):
    return pltpu.with_memory_space_constraint(value, pltpu.HBM)


def params(mib=28):
    return pltpu.CompilerParams(vmem_limit_bytes=mib << 20)


def cost(flops, bytes_accessed, transcendentals=0):
    return pl.CostEstimate(
        flops=flops, bytes_accessed=bytes_accessed, transcendentals=transcendentals
    )


def gelu_both(v):
    c, a = 0.7978845608028654, 0.044715
    sq = v * v
    t = jnp.tanh(c * v * (1.0 + a * sq))
    up = 0.5 * (1.0 + t)
    return v * up, up + 0.5 * v * (1.0 - t * t) * (c * (1.0 + 3.0 * a * sq))


def fill_rims(rimmed, block_ref, rim_ref):
    n = block_ref.shape[0]
    rimmed[0:RIM] = rim_ref[0:RIM]
    rimmed[RIM : RIM + n] = block_ref[...]
    rimmed[RIM + n : 2 * RIM + n] = rim_ref[RIM : 2 * RIM]


def conv_kernel(
    taps, x_ref, rim_ref, w_hbm, pooled_ref, even_hbm, odd_hbm, w_ref, rimmed, piece, wide, acc, slopes, sem, out_sem
):
    n, f = x_ref.shape
    copies = [
        pltpu.make_async_copy(w_hbm.at[k], w_ref.at[pl.ds(k * f, f)], sem.at[k])
        for k in range(taps)
    ]
    for copy in copies:
        copy.start()
    fill_rims(rimmed, x_ref, rim_ref)

    @pl.loop(0, n // PIECE)
    def _(m):
        r = pl.multiple_of(m * PIECE, PIECE)
        piece[...] = rimmed[pl.ds(r, PIECE + 2 * RIM), :].astype(F32)
        for k in range(taps):
            low = RIM - taps // 2 + k
            wide[pl.ds(r, PIECE), k * f : (k + 1) * f] = piece[low : low + PIECE, :].astype(BF)

    for copy in copies:
        copy.wait()

    @pl.loop(0, n // TILE)
    def _(m):
        r = pl.multiple_of(m * TILE, TILE)
        q = pl.ds(pl.multiple_of(m * (TILE // 2), TILE // 2), TILE // 2)
        total = jnp.dot(wide[pl.ds(r, TILE), :], w_ref[...], preferred_element_type=F32)
        for j in range(acc.shape[0]):
            cols = slice(j * LANES, (j + 1) * LANES)
            acc[j] = total[:, cols]
            even, even_slope = gelu_both(acc[j, pl.ds(0, TILE // 2, stride=2), :])
            odd, odd_slope = gelu_both(acc[j, pl.ds(1, TILE // 2, stride=2), :])
            pooled_ref[q, cols] = ((even + odd) * 0.5).astype(BF)
            slopes[0, q, cols] = even_slope * 0.5
            slopes[1, q, cols] = odd_slope * 0.5
        for side, out in enumerate((even_hbm, odd_hbm)):
            pltpu.make_async_copy(slopes.at[side, q], out.at[q], out_sem.at[side, m]).start()

    @pl.loop(0, n // TILE)
    def _(m):
        q = pl.ds(pl.multiple_of(m * (TILE // 2), TILE // 2), TILE // 2)
        for side, out in enumerate((even_hbm, odd_hbm)):
            pltpu.make_async_copy(slopes.at[side, q], out.at[q], out_sem.at[side, m]).wait()


def conv_pool(x, rim, w):
    taps, f, c = w.shape
    n = x.shape[0]
    return pl.pallas_call(
        functools.partial(conv_kernel, taps),
        out_shape=[jax.ShapeDtypeStruct((n // 2, c), BF)]
        + [pltpu.HBM((n // 2, c), F32)] * 2,
        in_specs=[IN_VMEM, IN_VMEM, IN_PLACE],
        out_specs=[IN_VMEM] + [pl.BlockSpec(memory_space=pltpu.HBM)] * 2,
        scratch_shapes=[
            VM((taps * f, c), BF),
            VM((n + 2 * RIM, f), BF),
            VM((PIECE + 2 * RIM, f), F32),
            VM((n, taps * f), BF),
            VM((c // LANES, TILE, LANES), F32),
            VM((2, n // 2, c), F32),
            pltpu.SemaphoreType.DMA((taps,)),
            pltpu.SemaphoreType.DMA((2, n // TILE)),
        ],
        compiler_params=params(),
        cost_estimate=cost(2 * n * f * c * taps, 2 * (n * f + taps * f * c) + 5 * n * c, n * c),
        name="conv_pool",
    )(x, rim, in_hbm(w))


def back_kernel(
    taps, g_ref, rim_ref, w_hbm, even_ref, odd_ref, order_ref, mine_ref, theirs_ref, w_ref, rimmed, piece, wide, pairs, flat, sem
):
    n = g_ref.shape[0]
    copies = [pltpu.make_async_copy(w_hbm.at[k], w_ref.at[k], sem.at[k]) for k in range(taps)]
    for copy in copies:
        copy.start()
    fill_rims(rimmed, g_ref, rim_ref)

    @pl.loop(0, n // PIECE)
    def _(m):
        r = pl.multiple_of(m * PIECE, PIECE)
        piece[...] = rimmed[pl.ds(r, PIECE + 2 * RIM), :].astype(F32)
        for k in range(taps):
            low = RIM + taps // 2 - k
            wide[k, pl.ds(r, PIECE), :] = piece[low : low + PIECE, :].astype(BF)

    for copy in copies:
        copy.wait()

    @pl.loop(0, n // TILE)
    def _(m):
        r = pl.multiple_of(m * TILE, TILE)
        rows = pl.ds(r, TILE)
        total = sum(
            lax.dot_general(
                wide[k, rows, :], w_ref[k], (((1,), (1,)), ((), ())), preferred_element_type=F32
            )
            for k in range(taps)
        )
        for j in range(pairs.shape[0]):
            cols = slice(j * LANES, (j + 1) * LANES)
            pairs[j, pl.ds(0, TILE, stride=2), :] = total[:, cols] * even_ref[rows, cols]
            pairs[j, pl.ds(1, TILE, stride=2), :] = total[:, cols] * odd_ref[rows, cols]
            flat[:, cols] = pairs[j].astype(BF)
        turned = lax.dot_general(
            order_ref[...], flat[...], (((1,), (1,)), ((), ())), preferred_element_type=F32
        )
        half = mine_ref.shape[0]
        cols = pl.ds(pl.multiple_of(2 * r, 2 * TILE), 2 * TILE)
        mine_ref[:, cols] = turned[:half].astype(BF)
        theirs_ref[:, cols] = turned[half:].astype(BF)


def conv_back(g, rim, w, even, odd, order):
    taps, f, c = w.shape
    n = g.shape[0]
    return pl.pallas_call(
        functools.partial(back_kernel, taps),
        out_shape=[jax.ShapeDtypeStruct((f // 2, 2 * n), BF)] * 2,
        in_specs=[IN_VMEM, IN_VMEM, IN_PLACE, IN_VMEM, IN_VMEM, IN_VMEM],
        out_specs=[IN_VMEM] * 2,
        scratch_shapes=[
            VM((taps, f, c), BF),
            VM((n + 2 * RIM, c), BF),
            VM((PIECE + 2 * RIM, c), F32),
            VM((taps, n, c), BF),
            VM((f // LANES, 2 * TILE, LANES), F32),
            VM((2 * TILE, f), BF),
            pltpu.SemaphoreType.DMA((taps,)),
        ],
        compiler_params=params(),
        cost_estimate=cost(
            2 * n * f * c * taps + 4 * n * f * f, 2 * (n * c + taps * f * c + f * f) + 12 * n * f
        ),
        name="conv_back",
    )(g, rim, in_hbm(w), even, odd, order)


def head_kernel(
    donor_ref, accept_ref, come_ref, head_ref, even_hbm, odd_hbm, order_hbm, g_ref, mine_ref, theirs_ref, slopes, order_ref, pairs, sem
):
    n = donor_ref.shape[0]
    copies = [
        pltpu.make_async_copy(even_hbm, slopes.at[0], sem.at[0]),
        pltpu.make_async_copy(odd_hbm, slopes.at[1], sem.at[1]),
        pltpu.make_async_copy(order_hbm, order_ref, sem.at[2]),
    ]
    for copy in copies:
        copy.start()
    slots, c = donor_ref.shape[1], come_ref.shape[2]
    each = come_ref.shape[1] // 2
    total = jnp.dot(
        donor_ref[...], come_ref[:, :each, :].reshape(slots, c), preferred_element_type=F32
    ) + jnp.dot(
        accept_ref[...], come_ref[:, each:, :].reshape(slots, c), preferred_element_type=F32
    )
    total = total * head_ref[...]
    for copy in copies:
        copy.wait()
    for j in range(pairs.shape[0]):
        cols = slice(j * LANES, (j + 1) * LANES)
        pairs[j, pl.ds(0, n, stride=2), :] = total[:, cols] * slopes[0, :, cols]
        pairs[j, pl.ds(1, n, stride=2), :] = total[:, cols] * slopes[1, :, cols]
        g_ref[:, cols] = pairs[j].astype(BF)
    turned = lax.dot_general(
        order_ref[...], g_ref[...], (((1,), (1,)), ((), ())), preferred_element_type=F32
    )
    half = mine_ref.shape[0]
    mine_ref[...] = turned[:half].astype(BF)
    theirs_ref[...] = turned[half:].astype(BF)


def head_back(donor, accept, come, head, even, odd, order):
    n, c = even.shape
    return pl.pallas_call(
        head_kernel,
        out_shape=[jax.ShapeDtypeStruct((2 * n, c), BF)]
        + [jax.ShapeDtypeStruct((c // 2, 2 * n), BF)] * 2,
        in_specs=[IN_VMEM] * 4 + [IN_PLACE] * 3,
        out_specs=[IN_VMEM] * 3,
        scratch_shapes=[
            VM((2, n, c), F32),
            VM((c, c), BF),
            VM((c // LANES, 2 * n, LANES), F32),
            pltpu.SemaphoreType.DMA((3,)),
        ],
        compiler_params=params(20),
        cost_estimate=cost(
            4 * n * c * donor.shape[1] + 4 * n * c * c, 2 * (come.size + c * c) + 16 * n * c
        ),
        name="head_back",
    )(donor, accept, come, head, in_hbm(even), in_hbm(odd), in_hbm(order))


def window_kernel(taps, own_ref, own_rim, other_ref, other_rim, out_ref, rimmed, piece):
    n = own_ref.shape[0]
    step = pl.program_id(0)

    @pl.when(step == 0)
    def _():
        fill_rims(rimmed.at[0], own_ref, own_rim)
        fill_rims(rimmed.at[1], other_ref, other_rim)

    per = n // PIECE
    side, m = step // per, step % per
    r = pl.multiple_of(m * PIECE, PIECE)
    piece[...] = rimmed[side, pl.ds(r, PIECE + 2 * RIM), :].astype(F32)
    for k in range(taps):
        low = RIM - taps // 2 + k
        out_ref[k] = piece[low : low + PIECE, :].astype(BF)


def windows_of(own, own_rim, other, other_rim, taps):
    n, f = own.shape
    return pl.pallas_call(
        functools.partial(window_kernel, taps),
        grid=(2 * n // PIECE,),
        out_shape=pltpu.HBM((taps, 2 * n, f), BF),
        in_specs=[IN_VMEM] * 4,
        out_specs=pl.BlockSpec((taps, PIECE, f), lambda i: (0, i, 0)),
        scratch_shapes=[VM((2, n + 2 * RIM, f), BF), VM((PIECE + 2 * RIM, f), F32)],
        compiler_params=params(14),
        cost_estimate=cost(0, 2 * (taps + 1) * 2 * n * f),
        name="windows",
    )(own, own_rim, other, other_rim)


def grad_kernel(mine_ref, got_ref, wide_ref, next_ref, far_ref, prev_ref, keep_ref, both):
    m, n = mine_ref.shape

    @pl.when(pl.program_id(0) == 0)
    def _():
        both[:, :n] = mine_ref[...]
        both[:, n:] = got_ref[...]

    total = jnp.dot(both[...], wide_ref[0], preferred_element_type=F32)
    q = m // 4
    keep_ref[0] = total[:q]
    next_ref[0] = total[q : 2 * q].astype(BF)
    far_ref[0] = total[2 * q : 3 * q].astype(BF)
    prev_ref[0] = total[3 * q :].astype(BF)


def grad_parts(mine, got, wide, first, taps):
    m, n = mine.shape
    f = wide.shape[2]
    block = lambda rows, low=0: pl.BlockSpec((1, rows, f), lambda k: (k + low, 0, 0))
    return pl.pallas_call(
        grad_kernel,
        grid=(taps,),
        out_shape=[jax.ShapeDtypeStruct((taps, m // 4, f), BF)] * 3
        + [jax.ShapeDtypeStruct((taps, m // 4, f), F32)],
        in_specs=[IN_VMEM, IN_VMEM, block(2 * n, first)],
        out_specs=[block(m // 4)] * 4,
        scratch_shapes=[VM((m, 2 * n), BF)],
        compiler_params=params(20),
        cost_estimate=cost(
            4 * m * n * f * taps, 2 * (2 * m * n + 2 * taps * n * f) + 3 * taps * m * f
        ),
        name="grad_parts",
    )(mine, got, in_hbm(wide))


def outer_rim(block, odd):
    return move(jnp.where(odd, block[-2:], block[:2]), OUTWARD)


def rim_of(odd, inner, outer):
    pad = jnp.zeros((RIM - 2, inner.shape[1]), inner.dtype)
    return jnp.concatenate(
        [pad, jnp.where(odd, inner, outer), jnp.where(odd, outer, inner), pad], axis=0
    )


def order_matrix(channels, seq):
    block = channels // N_SEQ
    core, x, z = seq % 2, (seq // 2) % NX, seq // (2 * NX)
    row = lax.broadcasted_iota(jnp.int32, (channels, 1), 0)
    half, r1, r2 = row // (16 * block), (row // (4 * block)) % 4, (row // block) % 4
    side = jnp.where(half == 0, core, 1 - core)
    to_x = (x + jnp.where(side == 0, r1, r2)) % NX
    to_z = (z + jnp.where(side == 0, r2, r1)) % NZ
    wanted = ((to_z * NX + to_x) * 2 + side) * block + row % block
    return (wanted == lax.broadcasted_iota(jnp.int32, (1, channels), 1)).astype(BF)


def axis_sum(after, far, prev, keep, ways):
    total = keep
    got = []
    for term, pairs in zip((far, after, prev), (ways[1], ways[0], ways[2])):
        got.append(move(term, pairs))
    for value in got:
        total = total + value.astype(F32)
    return total


def last_sum(total):
    b = total.shape[1] // 4
    terms = lax.optimization_barrier(
        tuple(total[:, r * b : (r + 1) * b].astype(BF) for r in (1, 2, 3))
    )
    return axis_sum(*terms, total[:, :b], WAYS[1])


def body(features, conv_one, conv_two, head_vector, owner_of, donor_row, accept_row, score_grad):
    seq = lax.axis_index("seq")
    odd = seq % 2 == 1
    taps = conv_one.shape[0]
    rows_one = features.shape[0]
    rows_two = rows_one // 2
    rows_c = rows_two // 2
    records = owner_of.shape[0]
    capacity = max(2, 2 * records // N_SEQ)
    slots = N_SEQ * capacity

    feat_outer = outer_rim(features, odd)
    feat_other = move(features, SIBLING)
    feat_rim = rim_of(odd, jnp.where(odd, feat_other[-2:], feat_other[:2]), feat_outer)
    owners = owner_of
    before = (owners == owners.reshape(1, records)) & (
        lax.broadcasted_iota(jnp.int32, (records, records), 1)
        < lax.broadcasted_iota(jnp.int32, (records, records), 0)
    )
    place = owners * capacity + jnp.sum(before.astype(jnp.int32), axis=1, keepdims=True)
    placed = (place == lax.broadcasted_iota(jnp.int32, (records, slots), 1)).astype(BF)
    told = jnp.stack([donor_row.astype(BF), score_grad], 0)
    sent = jnp.dot(told, placed, preferred_element_type=F32).astype(BF)
    sent = sent.reshape(2, N_SEQ, capacity).transpose(1, 0, 2)
    heard = lax.all_to_all(sent, "seq", split_axis=0, concat_axis=0, tiled=True)
    accepts = (
        accept_row[None, :] == lax.broadcasted_iota(jnp.int32, (rows_c, records), 0)
    ).astype(BF)
    accept_pick = jnp.dot(accepts, placed, preferred_element_type=F32).astype(BF)
    accept_add = jnp.dot(
        accepts * score_grad[None, :], placed, preferred_element_type=F32
    ).astype(BF)

    order_one = order_matrix(conv_one.shape[2], seq)
    order_two = order_matrix(conv_two.shape[2], seq)

    pooled, even_one, odd_one = conv_pool(features, feat_rim, conv_one)
    pool_outer = outer_rim(pooled, odd)
    pool_other = move(pooled, SIBLING)
    pool_rim = rim_of(odd, jnp.where(odd, pool_other[-2:], pool_other[:2]), pool_outer)
    embed, even_two, odd_two = conv_pool(pooled, pool_rim, conv_two)
    heard = lax.optimization_barrier((heard, pooled))[0]
    heard = heard.transpose(1, 0, 2).reshape(2, slots)
    donor_hit = heard[0:1].astype(F32) == lax.broadcasted_iota(
        jnp.int32, (rows_c, slots), 0
    ).astype(F32)
    donor_pick = donor_hit.astype(BF)
    donor_add = jnp.where(donor_hit, heard[1:2], jnp.zeros((), BF))
    pick = jnp.concatenate(
        [accept_pick.reshape(rows_c, N_SEQ, capacity), donor_pick.reshape(rows_c, N_SEQ, capacity)],
        axis=2,
    ).reshape(rows_c, 2 * slots)
    gone = lax.dot_general(
        pick, embed, (((0,), (0,)), ((), ())), preferred_element_type=F32
    ).astype(BF)
    come = lax.all_to_all(gone, "seq", split_axis=0, concat_axis=0, tiled=True)
    own, feat_other, outer, pool, pool_other, outer_two, _ = lax.optimization_barrier(
        (features, feat_other, feat_outer, pooled, pool_other, pool_outer, gone)
    )
    rim = rim_of(~odd, jnp.where(odd, own[:2], own[-2:]), move(outer, SIBLING))
    wide_one = windows_of(own, feat_rim, feat_other, rim, taps)
    rim = rim_of(~odd, jnp.where(odd, pool[:2], pool[-2:]), move(outer_two, SIBLING))
    wide_two = windows_of(pool, pool_rim, pool_other, rim, taps)
    come, wide_one, wide_two, order_one, order_two, donor_add, accept_add = (
        lax.optimization_barrier(
            (come, wide_one, wide_two, order_one, order_two, donor_add, accept_add)
        )
    )
    come = come.reshape(N_SEQ, 2 * capacity, come.shape[1])
    grads, mine_two, theirs_two = head_back(
        donor_add, accept_add, come, head_vector[None, :], even_two, odd_two, order_two
    )
    grad_rim = rim_of(
        odd, move(jnp.where(odd, grads[:2], grads[-2:]), SIBLING), outer_rim(grads, odd)
    )
    parts_two = grad_parts(mine_two, move(theirs_two, SIBLING), wide_two, 0, taps)
    grads = lax.optimization_barrier((grads, parts_two))[0]
    mine_one, theirs_one = conv_back(
        grads, grad_rim, conv_two, even_one, odd_one, order_one
    )
    got = move(theirs_one, SIBLING)
    cut = taps // 2 + 1
    parts_a = grad_parts(mine_one, got, wide_one, 0, cut)
    mine_one = lax.optimization_barrier((mine_one, parts_a))[0]
    parts_b = grad_parts(mine_one, got, wide_one, cut, taps - cut)
    grad_two = last_sum(axis_sum(*parts_two, WAYS[0])).transpose(1, 0, 2)
    sums_a = axis_sum(*parts_a, WAYS[0])
    sums_b = axis_sum(*parts_b, WAYS[0])
    sums = jnp.concatenate([sums_a, sums_b], axis=0)
    grad_one = last_sum(sums).transpose(1, 0, 2)
    return (grad_one, grad_two)


def solution(mesh):
    in_specs = (
        P(("dp", "seq"), None),
        P(),
        P(),
        P(),
        P(("dp", "seq"), None),
        P(("dp", "seq")),
        P(("dp", "seq")),
        P(("dp", "seq")),
    )
    out_specs = (P(("dp", "seq"), None, None), P(("dp", "seq"), None, None))

    return jax.shard_map(body, mesh=mesh, in_specs=in_specs, out_specs=out_specs, check_vma=False)
```

```python
import functools

import jax
import jax.numpy as jnp
from jax import lax
from jax.experimental import pallas as pl
from jax.experimental.pallas import tpu as pltpu
from jax.sharding import PartitionSpec as P


NZ, NX = 4, 4
BF = jnp.bfloat16
F32 = jnp.float32


def index_of(z, x, c):
    return ((z % NZ) * NX + (x % NX)) * 2 + c


def pairs_of(move):
    return [
        (index_of(z, x, c), index_of(*move(z, x, c)))
        for z in range(NZ)
        for x in range(NX)
        for c in range(2)
    ]


SIBLING = pairs_of(lambda z, x, c: (z, x, 1 - c))
WAYS = tuple(
    tuple(
        pairs_of(lambda z, x, c: (z, x + r, c) if c == first else (z + r, x, c)) for r in (1, 2, 3)
    )
    for first in (0, 1)
)
N_SEQ = NZ * NX * 2
OUTWARD = [(s, s - 1) for s in range(2, N_SEQ, 2)] + [(s, s + 1) for s in range(1, N_SEQ - 1, 2)]


def move(value, pairs):
    return lax.ppermute(value, "seq", pairs)


VM = pltpu.VMEM
IN_VMEM = pl.BlockSpec(memory_space=pltpu.VMEM)
IN_PLACE = pl.BlockSpec(memory_space=pl.ANY)
LANES = 128
PIECE = 128
TILE = 256
RIM = 16


def in_hbm(value):
    return pltpu.with_memory_space_constraint(value, pltpu.HBM)


def params(mib=28):
    return pltpu.CompilerParams(vmem_limit_bytes=mib << 20)


def cost(flops, bytes_accessed, transcendentals=0):
    return pl.CostEstimate(
        flops=flops, bytes_accessed=bytes_accessed, transcendentals=transcendentals
    )


def gelu_both(v):
    c, a = 0.7978845608028654, 0.044715
    sq = v * v
    t = jnp.tanh(c * v * (1.0 + a * sq))
    up = 0.5 * (1.0 + t)
    return v * up, up + 0.5 * v * (1.0 - t * t) * (c * (1.0 + 3.0 * a * sq))


def fill_rims(rimmed, block_ref, rim_ref):
    n = block_ref.shape[0]
    rimmed[0:RIM] = rim_ref[0:RIM]
    rimmed[RIM : RIM + n] = block_ref[...]
    rimmed[RIM + n : 2 * RIM + n] = rim_ref[RIM : 2 * RIM]


def conv_kernel(
    taps, x_hbm, rim_ref, w_hbm, pooled_ref, even_hbm, odd_hbm, w_ref, rimmed, piece, wide, acc, slopes, sem, out_sem
):
    n, f = x_hbm.shape
    block = pltpu.make_async_copy(x_hbm, rimmed.at[pl.ds(RIM, n)], sem.at[taps])
    block.start()
    copies = [
        pltpu.make_async_copy(w_hbm.at[k], w_ref.at[pl.ds(k * f, f)], sem.at[k])
        for k in range(taps)
    ]
    for copy in copies:
        copy.start()
    rimmed[0:RIM] = rim_ref[0:RIM]
    rimmed[RIM + n : 2 * RIM + n] = rim_ref[RIM : 2 * RIM]
    block.wait()

    @pl.loop(0, n // PIECE)
    def _(m):
        r = pl.multiple_of(m * PIECE, PIECE)
        piece[...] = rimmed[pl.ds(r, PIECE + 2 * RIM), :].astype(F32)
        for k in range(taps):
            low = RIM - taps // 2 + k
            wide[pl.ds(r, PIECE), k * f : (k + 1) * f] = piece[low : low + PIECE, :].astype(BF)

    for copy in copies:
        copy.wait()

    @pl.loop(0, n // TILE)
    def _(m):
        r = pl.multiple_of(m * TILE, TILE)
        q = pl.ds(pl.multiple_of(m * (TILE // 2), TILE // 2), TILE // 2)
        total = jnp.dot(wide[pl.ds(r, TILE), :], w_ref[...], preferred_element_type=F32)
        for j in range(acc.shape[0]):
            cols = slice(j * LANES, (j + 1) * LANES)
            acc[j] = total[:, cols]
            even, even_slope = gelu_both(acc[j, pl.ds(0, TILE // 2, stride=2), :])
            odd, odd_slope = gelu_both(acc[j, pl.ds(1, TILE // 2, stride=2), :])
            pooled_ref[q, cols] = ((even + odd) * 0.5).astype(BF)
            slopes[0, q, cols] = even_slope * 0.5
            slopes[1, q, cols] = odd_slope * 0.5
        for side, out in enumerate((even_hbm, odd_hbm)):
            pltpu.make_async_copy(slopes.at[side, q], out.at[q], out_sem.at[side, m]).start()

    @pl.loop(0, n // TILE)
    def _(m):
        q = pl.ds(pl.multiple_of(m * (TILE // 2), TILE // 2), TILE // 2)
        for side, out in enumerate((even_hbm, odd_hbm)):
            pltpu.make_async_copy(slopes.at[side, q], out.at[q], out_sem.at[side, m]).wait()


def conv_pool(x, rim, w):
    taps, f, c = w.shape
    n = x.shape[0]
    return pl.pallas_call(
        functools.partial(conv_kernel, taps),
        out_shape=[jax.ShapeDtypeStruct((n // 2, c), BF)]
        + [pltpu.HBM((n // 2, c), F32)] * 2,
        in_specs=[IN_PLACE, IN_VMEM, IN_PLACE],
        out_specs=[IN_VMEM] + [pl.BlockSpec(memory_space=pltpu.HBM)] * 2,
        scratch_shapes=[
            VM((taps * f, c), BF),
            VM((n + 2 * RIM, f), BF),
            VM((PIECE + 2 * RIM, f), F32),
            VM((n, taps * f), BF),
            VM((c // LANES, TILE, LANES), F32),
            VM((2, n // 2, c), F32),
            pltpu.SemaphoreType.DMA((taps + 1,)),
            pltpu.SemaphoreType.DMA((2, n // TILE)),
        ],
        compiler_params=params(),
        cost_estimate=cost(2 * n * f * c * taps, 2 * (n * f + taps * f * c) + 5 * n * c, n * c),
        name="conv_pool",
    )(x, rim, in_hbm(w))


def back_kernel(
    taps, g_ref, rim_ref, w_hbm, even_ref, odd_ref, order_ref, mine_ref, theirs_ref, w_ref, rimmed, piece, wide, pairs, flat, sem
):
    n = g_ref.shape[0]
    copies = [pltpu.make_async_copy(w_hbm.at[k], w_ref.at[k], sem.at[k]) for k in range(taps)]
    for copy in copies:
        copy.start()
    fill_rims(rimmed, g_ref, rim_ref)

    @pl.loop(0, n // PIECE)
    def _(m):
        r = pl.multiple_of(m * PIECE, PIECE)
        piece[...] = rimmed[pl.ds(r, PIECE + 2 * RIM), :].astype(F32)
        for k in range(taps):
            low = RIM + taps // 2 - k
            wide[k, pl.ds(r, PIECE), :] = piece[low : low + PIECE, :].astype(BF)

    for copy in copies:
        copy.wait()

    @pl.loop(0, n // TILE)
    def _(m):
        r = pl.multiple_of(m * TILE, TILE)
        rows = pl.ds(r, TILE)
        total = sum(
            lax.dot_general(
                wide[k, rows, :], w_ref[k], (((1,), (1,)), ((), ())), preferred_element_type=F32
            )
            for k in range(taps)
        )
        for j in range(pairs.shape[0]):
            cols = slice(j * LANES, (j + 1) * LANES)
            pairs[j, pl.ds(0, TILE, stride=2), :] = total[:, cols] * even_ref[rows, cols]
            pairs[j, pl.ds(1, TILE, stride=2), :] = total[:, cols] * odd_ref[rows, cols]
            flat[:, cols] = pairs[j].astype(BF)
        turned = lax.dot_general(
            order_ref[...], flat[...], (((1,), (1,)), ((), ())), preferred_element_type=F32
        )
        half = mine_ref.shape[0]
        cols = pl.ds(pl.multiple_of(2 * r, 2 * TILE), 2 * TILE)
        mine_ref[:, cols] = turned[:half].astype(BF)
        theirs_ref[:, cols] = turned[half:].astype(BF)


def conv_back(g, rim, w, even, odd, order):
    taps, f, c = w.shape
    n = g.shape[0]
    return pl.pallas_call(
        functools.partial(back_kernel, taps),
        out_shape=[jax.ShapeDtypeStruct((f // 2, 2 * n), BF)] * 2,
        in_specs=[IN_VMEM, IN_VMEM, IN_PLACE, IN_VMEM, IN_VMEM, IN_VMEM],
        out_specs=[IN_VMEM] * 2,
        scratch_shapes=[
            VM((taps, f, c), BF),
            VM((n + 2 * RIM, c), BF),
            VM((PIECE + 2 * RIM, c), F32),
            VM((taps, n, c), BF),
            VM((f // LANES, 2 * TILE, LANES), F32),
            VM((2 * TILE, f), BF),
            pltpu.SemaphoreType.DMA((taps,)),
        ],
        compiler_params=params(),
        cost_estimate=cost(
            2 * n * f * c * taps + 4 * n * f * f, 2 * (n * c + taps * f * c + f * f) + 12 * n * f
        ),
        name="conv_back",
    )(g, rim, in_hbm(w), even, odd, order)


def head_kernel(
    donor_ref, accept_ref, come_ref, head_ref, even_hbm, odd_hbm, order_hbm, g_ref, mine_ref, theirs_ref, slopes, order_ref, pairs, sem
):
    n = donor_ref.shape[0]
    copies = [
        pltpu.make_async_copy(even_hbm, slopes.at[0], sem.at[0]),
        pltpu.make_async_copy(odd_hbm, slopes.at[1], sem.at[1]),
        pltpu.make_async_copy(order_hbm, order_ref, sem.at[2]),
    ]
    for copy in copies:
        copy.start()
    slots, c = donor_ref.shape[1], come_ref.shape[2]
    each = come_ref.shape[1] // 2
    total = jnp.dot(
        donor_ref[...], come_ref[:, :each, :].reshape(slots, c), preferred_element_type=F32
    ) + jnp.dot(
        accept_ref[...], come_ref[:, each:, :].reshape(slots, c), preferred_element_type=F32
    )
    total = total * head_ref[...]
    for copy in copies:
        copy.wait()
    for j in range(pairs.shape[0]):
        cols = slice(j * LANES, (j + 1) * LANES)
        pairs[j, pl.ds(0, n, stride=2), :] = total[:, cols] * slopes[0, :, cols]
        pairs[j, pl.ds(1, n, stride=2), :] = total[:, cols] * slopes[1, :, cols]
        g_ref[:, cols] = pairs[j].astype(BF)
    turned = lax.dot_general(
        order_ref[...], g_ref[...], (((1,), (1,)), ((), ())), preferred_element_type=F32
    )
    half = mine_ref.shape[0]
    mine_ref[...] = turned[:half].astype(BF)
    theirs_ref[...] = turned[half:].astype(BF)


def head_back(donor, accept, come, head, even, odd, order):
    n, c = even.shape
    return pl.pallas_call(
        head_kernel,
        out_shape=[jax.ShapeDtypeStruct((2 * n, c), BF)]
        + [jax.ShapeDtypeStruct((c // 2, 2 * n), BF)] * 2,
        in_specs=[IN_VMEM] * 4 + [IN_PLACE] * 3,
        out_specs=[IN_VMEM] * 3,
        scratch_shapes=[
            VM((2, n, c), F32),
            VM((c, c), BF),
            VM((c // LANES, 2 * n, LANES), F32),
            pltpu.SemaphoreType.DMA((3,)),
        ],
        compiler_params=params(20),
        cost_estimate=cost(
            4 * n * c * donor.shape[1] + 4 * n * c * c, 2 * (come.size + c * c) + 16 * n * c
        ),
        name="head_back",
    )(donor, accept, come, head, in_hbm(even), in_hbm(odd), in_hbm(order))


def window_kernel(taps, own_ref, own_rim, other_ref, other_rim, out_ref, rimmed, piece):
    n = own_ref.shape[0]
    step = pl.program_id(0)

    @pl.when(step == 0)
    def _():
        fill_rims(rimmed.at[0], own_ref, own_rim)
        fill_rims(rimmed.at[1], other_ref, other_rim)

    per = n // PIECE
    side, m = step // per, step % per
    r = pl.multiple_of(m * PIECE, PIECE)
    piece[...] = rimmed[side, pl.ds(r, PIECE + 2 * RIM), :].astype(F32)
    for k in range(taps):
        low = RIM - taps // 2 + k
        out_ref[k] = piece[low : low + PIECE, :].astype(BF)


def windows_of(own, own_rim, other, other_rim, taps):
    n, f = own.shape
    return pl.pallas_call(
        functools.partial(window_kernel, taps),
        grid=(2 * n // PIECE,),
        out_shape=pltpu.HBM((taps, 2 * n, f), BF),
        in_specs=[IN_VMEM] * 4,
        out_specs=pl.BlockSpec((taps, PIECE, f), lambda i: (0, i, 0)),
        scratch_shapes=[VM((2, n + 2 * RIM, f), BF), VM((PIECE + 2 * RIM, f), F32)],
        compiler_params=params(14),
        cost_estimate=cost(0, 2 * (taps + 1) * 2 * n * f),
        name="windows",
    )(own, own_rim, other, other_rim)


def grad_kernel(mine_ref, got_ref, wide_ref, next_ref, far_ref, prev_ref, keep_ref, both):
    m, n = mine_ref.shape

    @pl.when(pl.program_id(0) == 0)
    def _():
        both[:, :n] = mine_ref[...]
        both[:, n:] = got_ref[...]

    total = jnp.dot(both[...], wide_ref[0], preferred_element_type=F32)
    q = m // 4
    keep_ref[0] = total[:q]
    next_ref[0] = total[q : 2 * q].astype(BF)
    far_ref[0] = total[2 * q : 3 * q].astype(BF)
    prev_ref[0] = total[3 * q :].astype(BF)


def grad_parts(mine, got, wide, first, taps):
    m, n = mine.shape
    f = wide.shape[2]
    block = lambda rows, low=0: pl.BlockSpec((1, rows, f), lambda k: (k + low, 0, 0))
    return pl.pallas_call(
        grad_kernel,
        grid=(taps,),
        out_shape=[jax.ShapeDtypeStruct((taps, m // 4, f), BF)] * 3
        + [jax.ShapeDtypeStruct((taps, m // 4, f), F32)],
        in_specs=[IN_VMEM, IN_VMEM, block(2 * n, first)],
        out_specs=[block(m // 4)] * 4,
        scratch_shapes=[VM((m, 2 * n), BF)],
        compiler_params=params(20),
        cost_estimate=cost(
            4 * m * n * f * taps, 2 * (2 * m * n + 2 * taps * n * f) + 3 * taps * m * f
        ),
        name="grad_parts",
    )(mine, got, in_hbm(wide))


def outer_rim(block, odd):
    return move(jnp.where(odd, block[-2:], block[:2]), OUTWARD)


def rim_of(odd, inner, outer):
    pad = jnp.zeros((RIM - 2, inner.shape[1]), inner.dtype)
    return jnp.concatenate(
        [pad, jnp.where(odd, inner, outer), jnp.where(odd, outer, inner), pad], axis=0
    )


def order_matrix(channels, seq):
    block = channels // N_SEQ
    core, x, z = seq % 2, (seq // 2) % NX, seq // (2 * NX)
    row = lax.broadcasted_iota(jnp.int32, (channels, 1), 0)
    half, r1, r2 = row // (16 * block), (row // (4 * block)) % 4, (row // block) % 4
    side = jnp.where(half == 0, core, 1 - core)
    to_x = (x + jnp.where(side == 0, r1, r2)) % NX
    to_z = (z + jnp.where(side == 0, r2, r1)) % NZ
    wanted = ((to_z * NX + to_x) * 2 + side) * block + row % block
    return (wanted == lax.broadcasted_iota(jnp.int32, (1, channels), 1)).astype(BF)


def axis_sum(after, far, prev, keep, ways):
    total = keep
    got = []
    for term, pairs in zip((far, after, prev), (ways[1], ways[0], ways[2])):
        got.append(move(term, pairs))
    for value in got:
        total = total + value.astype(F32)
    return total


def last_sum(total):
    b = total.shape[1] // 4
    terms = lax.optimization_barrier(
        tuple(total[:, r * b : (r + 1) * b].astype(BF) for r in (1, 2, 3))
    )
    return axis_sum(*terms, total[:, :b], WAYS[1])


def body(features, conv_one, conv_two, head_vector, owner_of, donor_row, accept_row, score_grad):
    seq = lax.axis_index("seq")
    odd = seq % 2 == 1
    taps = conv_one.shape[0]
    rows_one = features.shape[0]
    rows_two = rows_one // 2
    rows_c = rows_two // 2
    records = owner_of.shape[0]
    capacity = max(2, 2 * records // N_SEQ)
    slots = N_SEQ * capacity

    feat_outer = outer_rim(features, odd)
    feat_other = move(features, SIBLING)
    feat_rim = rim_of(odd, jnp.where(odd, feat_other[-2:], feat_other[:2]), feat_outer)
    owners = owner_of
    before = (owners == owners.reshape(1, records)) & (
        lax.broadcasted_iota(jnp.int32, (records, records), 1)
        < lax.broadcasted_iota(jnp.int32, (records, records), 0)
    )
    place = owners * capacity + jnp.sum(before.astype(jnp.int32), axis=1, keepdims=True)
    placed = (place == lax.broadcasted_iota(jnp.int32, (records, slots), 1)).astype(BF)
    told = jnp.stack([donor_row.astype(BF), score_grad], 0)
    sent = jnp.dot(told, placed, preferred_element_type=F32).astype(BF)
    sent = sent.reshape(2, N_SEQ, capacity).transpose(1, 0, 2)
    heard = lax.all_to_all(sent, "seq", split_axis=0, concat_axis=0, tiled=True)
    order_one = order_matrix(conv_one.shape[2], seq)
    order_two = order_matrix(conv_two.shape[2], seq)

    pooled, even_one, odd_one = conv_pool(in_hbm(features), feat_rim, conv_one)
    pool_outer = outer_rim(pooled, odd)
    pool_other = move(pooled, SIBLING)
    pool_rim = rim_of(odd, jnp.where(odd, pool_other[-2:], pool_other[:2]), pool_outer)
    embed, even_two, odd_two = conv_pool(pooled, pool_rim, conv_two)
    heard, placed, _ = lax.optimization_barrier((heard, placed, pooled))
    accepts = (
        accept_row[None, :] == lax.broadcasted_iota(jnp.int32, (rows_c, records), 0)
    ).astype(BF)
    accept_pick = jnp.dot(accepts, placed, preferred_element_type=F32).astype(BF)
    accept_add = jnp.dot(
        accepts * score_grad[None, :], placed, preferred_element_type=F32
    ).astype(BF)

    heard = heard.transpose(1, 0, 2).reshape(2, slots)
    donor_hit = heard[0:1].astype(F32) == lax.broadcasted_iota(
        jnp.int32, (rows_c, slots), 0
    ).astype(F32)
    donor_pick = donor_hit.astype(BF)
    donor_add = jnp.where(donor_hit, heard[1:2], jnp.zeros((), BF))
    pick = jnp.concatenate(
        [accept_pick.reshape(rows_c, N_SEQ, capacity), donor_pick.reshape(rows_c, N_SEQ, capacity)],
        axis=2,
    ).reshape(rows_c, 2 * slots)
    gone = lax.dot_general(
        pick, embed, (((0,), (0,)), ((), ())), preferred_element_type=F32
    ).astype(BF)
    come = lax.all_to_all(gone, "seq", split_axis=0, concat_axis=0, tiled=True)
    own, feat_other, outer, pool, pool_other, outer_two, _ = lax.optimization_barrier(
        (features, feat_other, feat_outer, pooled, pool_other, pool_outer, gone)
    )
    rim = rim_of(~odd, jnp.where(odd, own[:2], own[-2:]), move(outer, SIBLING))
    wide_one = windows_of(own, feat_rim, feat_other, rim, taps)
    rim = rim_of(~odd, jnp.where(odd, pool[:2], pool[-2:]), move(outer_two, SIBLING))
    wide_two = windows_of(pool, pool_rim, pool_other, rim, taps)
    come, wide_one, wide_two, order_one, order_two, donor_add, accept_add = (
        lax.optimization_barrier(
            (come, wide_one, wide_two, order_one, order_two, donor_add, accept_add)
        )
    )
    come = come.reshape(N_SEQ, 2 * capacity, come.shape[1])
    grads, mine_two, theirs_two = head_back(
        donor_add, accept_add, come, head_vector[None, :], even_two, odd_two, order_two
    )
    grad_rim = rim_of(
        odd, move(jnp.where(odd, grads[:2], grads[-2:]), SIBLING), outer_rim(grads, odd)
    )
    parts_two = grad_parts(mine_two, move(theirs_two, SIBLING), wide_two, 0, taps)
    grads = lax.optimization_barrier((grads, parts_two))[0]
    mine_one, theirs_one = conv_back(
        grads, grad_rim, conv_two, even_one, odd_one, order_one
    )
    got = move(theirs_one, SIBLING)
    cut = taps // 2 + 1
    parts_a = grad_parts(mine_one, got, wide_one, 0, cut)
    mine_one = lax.optimization_barrier((mine_one, parts_a))[0]
    parts_b = grad_parts(mine_one, got, wide_one, cut, taps - cut)
    grad_two = last_sum(axis_sum(*parts_two, WAYS[0])).transpose(1, 0, 2)
    sums_a = axis_sum(*parts_a, WAYS[0])
    sums_b = axis_sum(*parts_b, WAYS[0])
    sums = jnp.concatenate([sums_a, sums_b], axis=0)
    grad_one = last_sum(sums).transpose(1, 0, 2)
    return (grad_one, grad_two)


def solution(mesh):
    in_specs = (
        P(("dp", "seq"), None),
        P(),
        P(),
        P(),
        P(("dp", "seq"), None),
        P(("dp", "seq")),
        P(("dp", "seq")),
        P(("dp", "seq")),
    )
    out_specs = (P(("dp", "seq"), None, None), P(("dp", "seq"), None, None))

    return jax.shard_map(body, mesh=mesh, in_specs=in_specs, out_specs=out_specs, check_vma=False)
```

```python
import functools

import jax
import jax.numpy as jnp
from jax import lax
from jax.experimental import pallas as pl
from jax.experimental.pallas import tpu as pltpu
from jax.sharding import PartitionSpec as P


NZ, NX = 4, 4
BF = jnp.bfloat16
F32 = jnp.float32


def index_of(z, x, c):
    return ((z % NZ) * NX + (x % NX)) * 2 + c


def pairs_of(move):
    return [
        (index_of(z, x, c), index_of(*move(z, x, c)))
        for z in range(NZ)
        for x in range(NX)
        for c in range(2)
    ]


SIBLING = pairs_of(lambda z, x, c: (z, x, 1 - c))
WAYS = tuple(
    tuple(
        pairs_of(lambda z, x, c: (z, x + r, c) if c == first else (z + r, x, c)) for r in (1, 2, 3)
    )
    for first in (0, 1)
)
N_SEQ = NZ * NX * 2
OUTWARD = [(s, s - 1) for s in range(2, N_SEQ, 2)] + [(s, s + 1) for s in range(1, N_SEQ - 1, 2)]


def move(value, pairs):
    return lax.ppermute(value, "seq", pairs)


VM = pltpu.VMEM
IN_VMEM = pl.BlockSpec(memory_space=pltpu.VMEM)
IN_PLACE = pl.BlockSpec(memory_space=pl.ANY)
LANES = 128
PIECE = 128
TILE = 256
RIM = 16


def in_hbm(value):
    return pltpu.with_memory_space_constraint(value, pltpu.HBM)


def params(mib=28):
    return pltpu.CompilerParams(vmem_limit_bytes=mib << 20)


def cost(flops, bytes_accessed, transcendentals=0):
    return pl.CostEstimate(
        flops=flops, bytes_accessed=bytes_accessed, transcendentals=transcendentals
    )


def gelu_both(v):
    c, a = 0.7978845608028654, 0.044715
    sq = v * v
    up = 0.5 + 0.5 * jnp.tanh(v * (c + (c * a) * sq))
    out = v * up
    return out, 0.5 * up + out * (1.0 - up) * (c + (3.0 * a * c) * sq)


def fill_rims(rimmed, block_ref, rim_ref):
    n = block_ref.shape[0]
    rimmed[0:RIM] = rim_ref[0:RIM]
    rimmed[RIM : RIM + n] = block_ref[...]
    rimmed[RIM + n : 2 * RIM + n] = rim_ref[RIM : 2 * RIM]


def conv_kernel(
    taps, x_hbm, rim_ref, w_hbm, pooled_ref, even_hbm, odd_hbm, w_ref, rimmed, piece, wide, acc, slopes, sem, out_sem
):
    n, f = x_hbm.shape
    block = pltpu.make_async_copy(x_hbm, rimmed.at[pl.ds(RIM, n)], sem.at[taps])
    block.start()
    copies = [
        pltpu.make_async_copy(w_hbm.at[k], w_ref.at[pl.ds(k * f, f)], sem.at[k])
        for k in range(taps)
    ]
    for copy in copies:
        copy.start()
    rimmed[0:RIM] = rim_ref[0:RIM]
    rimmed[RIM + n : 2 * RIM + n] = rim_ref[RIM : 2 * RIM]
    block.wait()

    @pl.loop(0, n // PIECE)
    def _(m):
        r = pl.multiple_of(m * PIECE, PIECE)
        piece[...] = rimmed[pl.ds(r, PIECE + 2 * RIM), :].astype(F32)
        for k in range(taps):
            low = RIM - taps // 2 + k
            wide[pl.ds(r, PIECE), k * f : (k + 1) * f] = piece[low : low + PIECE, :].astype(BF)

    for copy in copies:
        copy.wait()

    def product(m):
        rows = pl.ds(pl.multiple_of(m * TILE, TILE), TILE)
        total = jnp.dot(wide[rows, :], w_ref[...], preferred_element_type=F32)
        for j in range(acc.shape[1]):
            acc[m % 2, j] = total[:, j * LANES : (j + 1) * LANES]

    def finish(m):
        q = pl.ds(pl.multiple_of(m * (TILE // 2), TILE // 2), TILE // 2)
        for j in range(acc.shape[1]):
            cols = slice(j * LANES, (j + 1) * LANES)
            even, even_slope = gelu_both(acc[m % 2, j, pl.ds(0, TILE // 2, stride=2), :])
            odd, odd_slope = gelu_both(acc[m % 2, j, pl.ds(1, TILE // 2, stride=2), :])
            pooled_ref[q, cols] = ((even + odd) * 0.5).astype(BF)
            slopes[0, q, cols] = even_slope
            slopes[1, q, cols] = odd_slope
        for side, out in enumerate((even_hbm, odd_hbm)):
            pltpu.make_async_copy(slopes.at[side, q], out.at[q], out_sem.at[side, m]).start()

    product(0)

    @pl.loop(1, n // TILE)
    def _(m):
        finish(m - 1)
        product(m)

    finish(n // TILE - 1)

    @pl.loop(0, n // TILE)
    def _(m):
        q = pl.ds(pl.multiple_of(m * (TILE // 2), TILE // 2), TILE // 2)
        for side, out in enumerate((even_hbm, odd_hbm)):
            pltpu.make_async_copy(slopes.at[side, q], out.at[q], out_sem.at[side, m]).wait()


def conv_pool(x, rim, w):
    taps, f, c = w.shape
    n = x.shape[0]
    return pl.pallas_call(
        functools.partial(conv_kernel, taps),
        out_shape=[jax.ShapeDtypeStruct((n // 2, c), BF)]
        + [pltpu.HBM((n // 2, c), F32)] * 2,
        in_specs=[IN_PLACE, IN_VMEM, IN_PLACE],
        out_specs=[IN_VMEM] + [pl.BlockSpec(memory_space=pltpu.HBM)] * 2,
        scratch_shapes=[
            VM((taps * f, c), BF),
            VM((n + 2 * RIM, f), BF),
            VM((PIECE + 2 * RIM, f), F32),
            VM((n, taps * f), BF),
            VM((2, c // LANES, TILE, LANES), F32),
            VM((2, n // 2, c), F32),
            pltpu.SemaphoreType.DMA((taps + 1,)),
            pltpu.SemaphoreType.DMA((2, n // TILE)),
        ],
        compiler_params=params(),
        cost_estimate=cost(2 * n * f * c * taps, 2 * (n * f + taps * f * c) + 5 * n * c, n * c),
        name="conv_pool",
    )(x, rim, in_hbm(w))


def back_kernel(
    taps, g_ref, rim_ref, w_hbm, even_ref, odd_ref, order_ref, mine_ref, theirs_ref, w_ref, rimmed, piece, wide, pairs, flat, sem
):
    n = g_ref.shape[0]
    copies = [pltpu.make_async_copy(w_hbm.at[k], w_ref.at[k], sem.at[k]) for k in range(taps)]
    for copy in copies:
        copy.start()
    fill_rims(rimmed, g_ref, rim_ref)

    @pl.loop(0, n // PIECE)
    def _(m):
        r = pl.multiple_of(m * PIECE, PIECE)
        piece[...] = rimmed[pl.ds(r, PIECE + 2 * RIM), :].astype(F32)
        for k in range(taps):
            low = RIM + taps // 2 - k
            wide[k, pl.ds(r, PIECE), :] = piece[low : low + PIECE, :].astype(BF)

    for copy in copies:
        copy.wait()

    @pl.loop(0, n // TILE)
    def _(m):
        r = pl.multiple_of(m * TILE, TILE)
        rows = pl.ds(r, TILE)
        total = sum(
            lax.dot_general(
                wide[k, rows, :], w_ref[k], (((1,), (1,)), ((), ())), preferred_element_type=F32
            )
            for k in range(taps)
        )
        for j in range(pairs.shape[0]):
            cols = slice(j * LANES, (j + 1) * LANES)
            pairs[j, pl.ds(0, TILE, stride=2), :] = total[:, cols] * even_ref[rows, cols]
            pairs[j, pl.ds(1, TILE, stride=2), :] = total[:, cols] * odd_ref[rows, cols]
            flat[:, cols] = pairs[j].astype(BF)
        turned = lax.dot_general(
            order_ref[...], flat[...], (((1,), (1,)), ((), ())), preferred_element_type=F32
        )
        half = mine_ref.shape[0]
        cols = pl.ds(pl.multiple_of(2 * r, 2 * TILE), 2 * TILE)
        mine_ref[:, cols] = turned[:half].astype(BF)
        theirs_ref[:, cols] = turned[half:].astype(BF)


def conv_back(g, rim, w, even, odd, order):
    taps, f, c = w.shape
    n = g.shape[0]
    return pl.pallas_call(
        functools.partial(back_kernel, taps),
        out_shape=[jax.ShapeDtypeStruct((f // 2, 2 * n), BF)] * 2,
        in_specs=[IN_VMEM, IN_VMEM, IN_PLACE, IN_VMEM, IN_VMEM, IN_VMEM],
        out_specs=[IN_VMEM] * 2,
        scratch_shapes=[
            VM((taps, f, c), BF),
            VM((n + 2 * RIM, c), BF),
            VM((PIECE + 2 * RIM, c), F32),
            VM((taps, n, c), BF),
            VM((f // LANES, 2 * TILE, LANES), F32),
            VM((2 * TILE, f), BF),
            pltpu.SemaphoreType.DMA((taps,)),
        ],
        compiler_params=params(),
        cost_estimate=cost(
            2 * n * f * c * taps + 4 * n * f * f, 2 * (n * c + taps * f * c + f * f) + 12 * n * f
        ),
        name="conv_back",
    )(g, rim, in_hbm(w), even, odd, order)


def head_kernel(
    donor_ref, accept_ref, come_ref, head_ref, even_hbm, odd_hbm, order_hbm, g_ref, mine_ref, theirs_ref, slopes, order_ref, pairs, sem
):
    n = donor_ref.shape[0]
    copies = [
        pltpu.make_async_copy(even_hbm, slopes.at[0], sem.at[0]),
        pltpu.make_async_copy(odd_hbm, slopes.at[1], sem.at[1]),
        pltpu.make_async_copy(order_hbm, order_ref, sem.at[2]),
    ]
    for copy in copies:
        copy.start()
    slots, c = donor_ref.shape[1], come_ref.shape[2]
    each = come_ref.shape[1] // 2
    total = jnp.dot(
        donor_ref[...], come_ref[:, :each, :].reshape(slots, c), preferred_element_type=F32
    ) + jnp.dot(
        accept_ref[...], come_ref[:, each:, :].reshape(slots, c), preferred_element_type=F32
    )
    total = total * head_ref[...]
    copies[0].wait()
    copies[1].wait()
    for j in range(pairs.shape[0]):
        cols = slice(j * LANES, (j + 1) * LANES)
        pairs[j, pl.ds(0, n, stride=2), :] = total[:, cols] * slopes[0, :, cols]
        pairs[j, pl.ds(1, n, stride=2), :] = total[:, cols] * slopes[1, :, cols]
        g_ref[:, cols] = pairs[j].astype(BF)
    copies[2].wait()
    turned = lax.dot_general(
        order_ref[...], g_ref[...], (((1,), (1,)), ((), ())), preferred_element_type=F32
    )
    half = mine_ref.shape[0]
    mine_ref[...] = turned[:half].astype(BF)
    theirs_ref[...] = turned[half:].astype(BF)


def head_back(donor, accept, come, head, even, odd, order):
    n, c = even.shape
    return pl.pallas_call(
        head_kernel,
        out_shape=[jax.ShapeDtypeStruct((2 * n, c), BF)]
        + [jax.ShapeDtypeStruct((c // 2, 2 * n), BF)] * 2,
        in_specs=[IN_VMEM] * 4 + [IN_PLACE] * 3,
        out_specs=[IN_VMEM] * 3,
        scratch_shapes=[
            VM((2, n, c), F32),
            VM((c, c), BF),
            VM((c // LANES, 2 * n, LANES), F32),
            pltpu.SemaphoreType.DMA((3,)),
        ],
        compiler_params=params(20),
        cost_estimate=cost(
            4 * n * c * donor.shape[1] + 4 * n * c * c, 2 * (come.size + c * c) + 16 * n * c
        ),
        name="head_back",
    )(donor, accept, come, head, in_hbm(even), in_hbm(odd), in_hbm(order))


def window_kernel(taps, own_ref, own_rim, other_ref, other_rim, out_ref, rimmed, piece):
    n = own_ref.shape[0]
    step = pl.program_id(0)

    @pl.when(step == 0)
    def _():
        fill_rims(rimmed.at[0], own_ref, own_rim)
        fill_rims(rimmed.at[1], other_ref, other_rim)

    per = n // PIECE
    side, m = step // per, step % per
    r = pl.multiple_of(m * PIECE, PIECE)
    piece[...] = rimmed[side, pl.ds(r, PIECE + 2 * RIM), :].astype(F32)
    for k in range(taps):
        low = RIM - taps // 2 + k
        out_ref[k] = piece[low : low + PIECE, :].astype(BF)


def windows_of(own, own_rim, other, other_rim, taps):
    n, f = own.shape
    return pl.pallas_call(
        functools.partial(window_kernel, taps),
        grid=(2 * n // PIECE,),
        out_shape=pltpu.HBM((taps, 2 * n, f), BF),
        in_specs=[IN_VMEM] * 4,
        out_specs=pl.BlockSpec((taps, PIECE, f), lambda i: (0, i, 0)),
        scratch_shapes=[VM((2, n + 2 * RIM, f), BF), VM((PIECE + 2 * RIM, f), F32)],
        compiler_params=params(14),
        cost_estimate=cost(0, 2 * (taps + 1) * 2 * n * f),
        name="windows",
    )(own, own_rim, other, other_rim)


def grad_kernel(mine_ref, got_ref, wide_ref, next_ref, far_ref, prev_ref, keep_ref, both):
    m, n = mine_ref.shape

    @pl.when(pl.program_id(0) == 0)
    def _():
        both[:, :n] = mine_ref[...]
        both[:, n:] = got_ref[...]

    total = jnp.dot(both[...], wide_ref[0], preferred_element_type=F32)
    q = m // 4
    keep_ref[0] = total[:q]
    next_ref[0] = total[q : 2 * q].astype(BF)
    far_ref[0] = total[2 * q : 3 * q].astype(BF)
    prev_ref[0] = total[3 * q :].astype(BF)


def grad_parts(mine, got, wide, first, taps):
    m, n = mine.shape
    f = wide.shape[2]
    block = lambda rows, low=0: pl.BlockSpec((1, rows, f), lambda k: (k + low, 0, 0))
    return pl.pallas_call(
        grad_kernel,
        grid=(taps,),
        out_shape=[jax.ShapeDtypeStruct((taps, m // 4, f), BF)] * 3
        + [jax.ShapeDtypeStruct((taps, m // 4, f), F32)],
        in_specs=[IN_VMEM, IN_VMEM, block(2 * n, first)],
        out_specs=[block(m // 4)] * 4,
        scratch_shapes=[VM((m, 2 * n), BF)],
        compiler_params=params(20),
        cost_estimate=cost(
            4 * m * n * f * taps, 2 * (2 * m * n + 2 * taps * n * f) + 3 * taps * m * f
        ),
        name="grad_parts",
    )(mine, got, in_hbm(wide))


def outer_rim(block, odd):
    return move(jnp.where(odd, block[-2:], block[:2]), OUTWARD)


def rim_of(odd, inner, outer):
    pad = jnp.zeros((RIM - 2, inner.shape[1]), inner.dtype)
    return jnp.concatenate(
        [pad, jnp.where(odd, inner, outer), jnp.where(odd, outer, inner), pad], axis=0
    )


def order_matrix(channels, seq):
    block = channels // N_SEQ
    core, x, z = seq % 2, (seq // 2) % NX, seq // (2 * NX)
    row = lax.broadcasted_iota(jnp.int32, (channels, 1), 0)
    half, r1, r2 = row // (16 * block), (row // (4 * block)) % 4, (row // block) % 4
    side = jnp.where(half == 0, core, 1 - core)
    to_x = (x + jnp.where(side == 0, r1, r2)) % NX
    to_z = (z + jnp.where(side == 0, r2, r1)) % NZ
    wanted = ((to_z * NX + to_x) * 2 + side) * block + row % block
    return (wanted == lax.broadcasted_iota(jnp.int32, (1, channels), 1)).astype(BF)


def axis_sum(after, far, prev, keep, ways):
    total = keep
    got = []
    for term, pairs in zip((far, after, prev), (ways[1], ways[0], ways[2])):
        got.append(move(term, pairs))
    for value in got:
        total = total + value.astype(F32)
    return total


def last_sum(total):
    b = total.shape[1] // 4
    terms = lax.optimization_barrier(
        tuple(total[:, r * b : (r + 1) * b].astype(BF) for r in (1, 2, 3))
    )
    return axis_sum(*terms, total[:, :b], WAYS[1])


def body(features, conv_one, conv_two, head_vector, owner_of, donor_row, accept_row, score_grad):
    seq = lax.axis_index("seq")
    odd = seq % 2 == 1
    taps = conv_one.shape[0]
    rows_one = features.shape[0]
    rows_two = rows_one // 2
    rows_c = rows_two // 2
    records = owner_of.shape[0]
    capacity = max(2, 2 * records // N_SEQ)
    slots = N_SEQ * capacity

    feat_outer = outer_rim(features, odd)
    feat_other = move(features, SIBLING)
    feat_rim = rim_of(odd, jnp.where(odd, feat_other[-2:], feat_other[:2]), feat_outer)
    owners = owner_of
    before = (owners == owners.reshape(1, records)) & (
        lax.broadcasted_iota(jnp.int32, (records, records), 1)
        < lax.broadcasted_iota(jnp.int32, (records, records), 0)
    )
    place = owners * capacity + jnp.sum(before.astype(jnp.int32), axis=1, keepdims=True)
    placed = (place == lax.broadcasted_iota(jnp.int32, (records, slots), 1)).astype(BF)
    told = jnp.stack([donor_row.astype(BF), score_grad], 0)
    sent = jnp.dot(told, placed, preferred_element_type=F32).astype(BF)
    sent = sent.reshape(2, N_SEQ, capacity).transpose(1, 0, 2)
    heard = lax.all_to_all(sent, "seq", split_axis=0, concat_axis=0, tiled=True)
    order_one = order_matrix(conv_one.shape[2], seq)
    order_two = order_matrix(conv_two.shape[2], seq)

    pooled, even_one, odd_one = conv_pool(in_hbm(features), feat_rim, conv_one)
    pool_outer = outer_rim(pooled, odd)
    pool_other = move(pooled, SIBLING)
    pool_rim = rim_of(odd, jnp.where(odd, pool_other[-2:], pool_other[:2]), pool_outer)
    embed, even_two, odd_two = conv_pool(pooled, pool_rim, conv_two)
    heard, placed, _ = lax.optimization_barrier((heard, placed, pooled))
    accepts = (
        accept_row[None, :] == lax.broadcasted_iota(jnp.int32, (rows_c, records), 0)
    ).astype(BF)
    accept_pick = jnp.dot(accepts, placed, preferred_element_type=F32).astype(BF)
    accept_add = jnp.dot(
        accepts * score_grad[None, :], placed, preferred_element_type=F32
    ).astype(BF)

    heard = heard.transpose(1, 0, 2).reshape(2, slots)
    donor_hit = heard[0:1].astype(F32) == lax.broadcasted_iota(
        jnp.int32, (rows_c, slots), 0
    ).astype(F32)
    donor_pick = donor_hit.astype(BF)
    donor_add = jnp.where(donor_hit, heard[1:2], jnp.zeros((), BF))
    pick = jnp.concatenate(
        [accept_pick.reshape(rows_c, N_SEQ, capacity), donor_pick.reshape(rows_c, N_SEQ, capacity)],
        axis=2,
    ).reshape(rows_c, 2 * slots)
    gone = lax.dot_general(
        pick, embed, (((0,), (0,)), ((), ())), preferred_element_type=F32
    ).astype(BF)
    come = lax.all_to_all(gone, "seq", split_axis=0, concat_axis=0, tiled=True)
    own, feat_other, outer, pool, pool_other, outer_two, _ = lax.optimization_barrier(
        (features, feat_other, feat_outer, pooled, pool_other, pool_outer, gone)
    )
    rim = rim_of(~odd, jnp.where(odd, own[:2], own[-2:]), move(outer, SIBLING))
    wide_one = windows_of(own, feat_rim, feat_other, rim, taps)
    rim = rim_of(~odd, jnp.where(odd, pool[:2], pool[-2:]), move(outer_two, SIBLING))
    wide_two = windows_of(pool, pool_rim, pool_other, rim, taps)
    come, wide_one, wide_two, order_one, order_two, donor_add, accept_add = (
        lax.optimization_barrier(
            (come, wide_one, wide_two, order_one, order_two, donor_add, accept_add)
        )
    )
    come = come.reshape(N_SEQ, 2 * capacity, come.shape[1])
    grads, mine_two, theirs_two = head_back(
        donor_add, accept_add, come, head_vector[None, :], even_two, odd_two, order_two
    )
    grad_rim = rim_of(
        odd, move(jnp.where(odd, grads[:2], grads[-2:]), SIBLING), outer_rim(grads, odd)
    )
    parts_two = grad_parts(mine_two, move(theirs_two, SIBLING), wide_two, 0, taps)
    grads = lax.optimization_barrier((grads, parts_two))[0]
    mine_one, theirs_one = conv_back(
        grads, grad_rim, conv_two, even_one, odd_one, order_one
    )
    got = move(theirs_one, SIBLING)
    cut = taps // 2 + 1
    parts_a = grad_parts(mine_one, got, wide_one, 0, cut)
    mine_one = lax.optimization_barrier((mine_one, parts_a))[0]
    parts_b = grad_parts(mine_one, got, wide_one, cut, taps - cut)
    grad_two = last_sum(axis_sum(*parts_two, WAYS[0])).transpose(1, 0, 2)
    sums_a = axis_sum(*parts_a, WAYS[0])
    sums_b = axis_sum(*parts_b, WAYS[0])
    sums = jnp.concatenate([sums_a, sums_b], axis=0)
    grad_one = last_sum(sums).transpose(1, 0, 2)
    return (grad_one, grad_two)


def solution(mesh):
    in_specs = (
        P(("dp", "seq"), None),
        P(),
        P(),
        P(),
        P(("dp", "seq"), None),
        P(("dp", "seq")),
        P(("dp", "seq")),
        P(("dp", "seq")),
    )
    out_specs = (P(("dp", "seq"), None, None), P(("dp", "seq"), None, None))

    return jax.shard_map(body, mesh=mesh, in_specs=in_specs, out_specs=out_specs, check_vma=False)
```
